32 devices in a mesh: slab: 8 (over y, x, core), wide: 4 (over z).
Axes of the slice: x: 2, y: 2, z: 4, core: 2. Of those that a mesh axis runs over, the one named last changes fastest.
Arguments:
- face_owner_state: bfloat16 [256, 16, 128], P(('slab', 'wide')), may hold values from -6 to 6
- face_neighbour_state: bfloat16 [256, 16, 128], P(('slab', 'wide')), may hold values from -6 to 6
- flux_linear: float32 [16, 16], replicated, may hold values from -1.5 to 1.5
- flux_quadratic: bfloat16 [16, 256], replicated, may hold values from -0.375 to 0.375
- species_weight: float32 [11], replicated, may hold values from 0.5 to 1.5
- cell_state: bfloat16 [512, 16, 128], P(('slab', 'wide')), may hold values from -6 to 6
- cell_tau: float32 [512, 128], P(('slab', 'wide')), may hold values from 0.5 to 4
- cell_rate: float32 [512, 128], P(('slab', 'wide')), may hold values from 0.5 to 2
- newton_residual: float32 [512, 16, 128], P(('slab', 'wide')), may hold values from -6 to 6
- tile_dest: int32 [256, 1], P(('slab', 'wide')), may hold values from 0 to 3; in each aligned block of 8 rows (0 to 7, 8 to 15, ...) at most 4 rows name the same one
- tile_row: int32 [256], P(('slab', 'wide')), may hold values from 0 to 15
- tile_nbr: int32 [256], P(('slab', 'wide')), may hold values from 0 to 23
- halo_list: int32 [32, 2, 4], P(('slab', 'wide')), may hold values from 0 to 15
Outputs:
- first_product: float32 [512, 16, 128], P(('slab', 'wide'))
- second_product: float32 [512, 16, 128], P(('slab', 'wide'))
The draws below stay inside these ranges and needn't reach their ends.
Inputs may be any that keep to these rules, and one draw needn't show every extreme that they name: `tile_dest`: among the face tiles of one device no owner is named more than 4 times, and in some device some owner is named exactly 4 times.
All inputs are finite; a program needn't handle non-finite values.
Results may differ from the reference program's by a relative error of at most 0.008.
Values may be sent and summed in bfloat16 or wider, within the bound.
A program may use at most 64 MiB of HBM per device.

```python
import math
import jax
import jax.numpy as jnp
import numpy as np
from jax import lax

VARS = 16
SPECIES = 11
TILE = 128
RD = 16
CAP = 4
HALO = 4
OWNERS = 4
FT = 8
ROWS = 512
TILES = 256
N_SLAB = 8
N_WIDE = 4


def set_ends(drawn, stream_key, smallest, top_value):
    longest = drawn.shape.index(max(drawn.shape))
    spots = []
    for shift in (0, 1):
        where = [jax.random.randint(jax.random.fold_in(stream_key, axis), (), 0, length) for axis, length in enumerate(drawn.shape)]
        where[longest] = (where[longest] + shift) % drawn.shape[longest]
        spots.append(tuple(where))
    return drawn.at[spots[0]].set(smallest).at[spots[1]].set(top_value)


def block_levels(rng, extent, pieces, least, high):
    gain, own = 1.0, jax.random.fold_in(rng, 6)
    for axis_at, blocks in pieces:
        draws = jnp.exp(jax.random.uniform(jax.random.fold_in(own, axis_at), (blocks,), jnp.float32, least / len(pieces), high / len(pieces)))
        gain = gain * jnp.repeat(draws, extent[axis_at] // blocks).reshape([-1 if axis == axis_at else 1 for axis in range(len(extent))])
    return gain


def assign_block(key, own, number, rows, amount, top, limit, lean):
    ranking = jax.random.permutation(key, amount)
    packed, ordinary = load_shares(amount, rows * top, limit, lean, True), load_shares(amount, rows * top, limit, lean, False)
    places = jnp.arange(amount)

    def named(lengths, offset_by):
        used = int((lengths > 0).sum())
        fixed = max(1, used // 4)
        passed = fixed + (places - fixed + offset_by * (used - fixed)) % max(1, amount - fixed)
        return jnp.zeros((amount,), jnp.int32).at[ranking[jnp.where(places < fixed, places, passed)]].set(jnp.asarray(lengths, jnp.int32))

    lengths = jnp.where(number % 4 == 0, named(packed, number // 4), named(ordinary, number - number // 4 - 1))
    mixed = jax.random.permutation(jax.random.fold_in(own, 3), amount)
    donor, receiver = mixed[0:amount // 2 * 2:2], mixed[1:amount // 2 * 2:2]
    slack = jnp.minimum(lengths[donor] - 1, limit - lengths[receiver]) // 2
    slack = jnp.where((donor == ranking[0]) | (receiver == ranking[0]) | (lengths[receiver] == 0), 0, jnp.maximum(slack, 0))
    passed = jax.random.randint(jax.random.fold_in(own, 4), (amount // 2,), 0, 1 << 20) % (slack + 1)
    lengths = lengths.at[donor].add(-passed).at[receiver].add(passed)
    items = jnp.searchsorted(jnp.cumsum(lengths), jnp.arange(rows * top), side="right").astype(jnp.int32)
    listing = items.reshape(top, rows).T
    listing = listing[jax.random.permutation(jax.random.fold_in(own, 1), rows)]
    offset_by = jax.random.randint(jax.random.fold_in(own, 2), (rows, 1), 0, top)
    return jnp.take_along_axis(listing, (jnp.arange(top)[None, :] + offset_by) % top, axis=1)


def load_shares(amount, total, most, lean, full):
    portions = [(1 << 20) // math.isqrt(rank ** lean) + 1 for rank in range(1, amount + 1)]
    largest = most if full else min(most, max(-(-total // amount), total * portions[0] // sum(portions)))
    least = 1 if total - largest >= amount - 1 else 0
    given, surplus = [largest] + [least] * (amount - 1), total - largest - least * (amount - 1)
    while surplus > 0:
        free = [i for i in range(1, amount) if given[i] < largest] or [i for i in range(1, amount) if given[i] < most]
        mass, remaining = sum([portions[i] for i in free]), surplus
        for i in free:
            extra = min(most - given[i], max(1, remaining * portions[i] // mass), surplus)
            given[i] = given[i] + extra
            surplus = surplus - extra
    return np.array(given)


def gaussian(stream_key, extent, scale, limit, split=(), kind=jnp.bfloat16):
    drawn = scale * jax.random.normal(stream_key, extent, jnp.float32)
    if split:
        drawn = drawn * block_levels(stream_key, extent, split, -0.22, 0.18)
    return jnp.clip(drawn, -limit, limit).astype(kind)


def setup_inputs(seed: int = 0) -> dict:
    key_of = jax.random.split(jax.random.key(seed), 14)
    face_owner_state = gaussian(key_of[0], (TILES, VARS, TILE), 1.0, 6.0, ((0, 32),))
    face_neighbour_state = gaussian(key_of[1], (TILES, VARS, TILE), 1.0, 6.0, ((0, 32),))
    flux_linear = gaussian(key_of[2], (VARS, VARS), VARS ** -0.5, 1.5, (), jnp.float32)
    flux_quadratic = gaussian(key_of[3], (VARS, VARS * VARS), (VARS * VARS) ** -0.5, 0.375)
    species_weight = jnp.clip(jax.random.uniform(key_of[4], (SPECIES,), jnp.float32, 0.5, 1.5), 0.5, 1.5)
    cell_state = gaussian(key_of[5], (ROWS, VARS, TILE), 1.0, 6.0, ((0, 32),))
    cell_tau = jnp.clip(jnp.exp(math.log(4.0) - 2.0794415 * jax.random.uniform(key_of[6], (ROWS, TILE), jnp.float32) ** block_levels(key_of[6], (ROWS, TILE), ((0, 32),), -0.2, 0.2)), 0.5, 4.0)
    cell_rate = jnp.clip(jnp.exp(math.log(2.0) - 1.3862944 * jax.random.uniform(key_of[7], (ROWS, TILE), jnp.float32) ** block_levels(key_of[7], (ROWS, TILE), ((0, 32),), -0.2, 0.2)), 0.5, 2.0)
    newton_residual = gaussian(key_of[8], (ROWS, VARS, TILE), 1.0, 6.0, ((0, 32),), jnp.float32)
    tile_dest_keys = jax.random.split(jax.random.fold_in(key_of[9], 1), TILES // FT)
    tile_dest_turns = jax.random.permutation(jax.random.fold_in(key_of[9], 3), TILES // FT)
    tile_dest = jax.vmap(lambda own, number: assign_block(jax.random.fold_in(key_of[9], 2), own, number, FT, OWNERS, 1, CAP, 2))(tile_dest_keys, tile_dest_turns).reshape((TILES, 1))
    tile_row = set_ends(jax.random.randint(key_of[10], (TILES,), 0, RD), jax.random.fold_in(key_of[10], 1), 0, RD - 1).astype(jnp.int32)
    tile_nbr = set_ends(jax.random.randint(key_of[11], (TILES,), 0, RD + 2 * HALO), jax.random.fold_in(key_of[11], 1), 0, (RD + 2 * HALO) - 1).astype(jnp.int32)
    halo_list = set_ends(jax.random.randint(key_of[12], (N_SLAB * N_WIDE, 2, HALO), 0, RD), jax.random.fold_in(key_of[12], 1), 0, RD - 1).astype(jnp.int32)
    return dict(face_owner_state=face_owner_state, face_neighbour_state=face_neighbour_state, flux_linear=flux_linear, flux_quadratic=flux_quadratic, species_weight=species_weight, cell_state=cell_state, cell_tau=cell_tau, cell_rate=cell_rate, newton_residual=newton_residual, tile_dest=tile_dest, tile_row=tile_row, tile_nbr=tile_nbr, halo_list=halo_list)


def assemble(owner_state, neighbour_state, flux_linear, flux_quadratic):
    count, width, tile = owner_state.shape
    own_f = owner_state.astype(jnp.float32)
    nbr_f = neighbour_state.astype(jnp.float32)
    quad = flux_quadratic.astype(jnp.float32)

    def jacobian(state):
        grown = jnp.einsum('kq,tkc->tqc', quad, state)
        return grown.reshape(count, width, width, tile) + flux_linear[None, :, :, None]
    speed = 1.0 + jnp.sqrt(0.5 * lax.optimization_barrier(jnp.mean(own_f * own_f + nbr_f * nbr_f, axis=1)))
    wave = speed[:, None, None, :] * jnp.eye(width, dtype=jnp.float32)[None, :, :, None]
    p_block = (0.5 * (jacobian(own_f) + wave)).astype(jnp.bfloat16)
    q_block = (0.5 * (jacobian(nbr_f) - wave)).astype(jnp.bfloat16)
    return jnp.stack([p_block, q_block], axis=1)

def source_product(vb, cell_state, cell_tau, cell_rate, species_weight):
    state = cell_state.astype(jnp.float32)
    vf = vb.astype(jnp.float32)
    nspec = species_weight.shape[0]
    rho = lax.optimization_barrier(jnp.sum(species_weight[None, :, None] * state[:, :nspec], axis=1))
    gap = state[:, 14] - state[:, 15]
    along = lax.optimization_barrier(jnp.sum(species_weight[None, :, None] * vf[:, :nspec], axis=1)) * gap + rho * (vf[:, 14] - vf[:, 15])
    change = along / cell_tau
    result = cell_rate[:, None, :] * vf
    result = result.at[:, 14].add(change)
    result = result.at[:, 15].add(-change)
    return result

def reference(face_owner_state, face_neighbour_state, flux_linear, flux_quadratic, species_weight, cell_state, cell_tau, cell_rate, newton_residual, tile_dest, tile_row, tile_nbr, halo_list):
    devices = N_SLAB * N_WIDE
    width = face_owner_state.shape[1]
    tile = face_owner_state.shape[2]
    owner_groups = face_owner_state.reshape(devices, FT, width, tile)
    nbr_groups = face_neighbour_state.reshape(devices, FT, width, tile)

    def build(pair):
        return assemble(pair[0], pair[1], flux_linear, flux_quadratic)
    blocks = lax.map(build, (owner_groups, nbr_groups))
    index = jnp.arange(devices * FT, dtype=jnp.int32)
    slab = index // FT // N_WIDE
    dest = tile_dest[:, 0].astype(jnp.int32)
    home = slab * N_WIDE + dest
    own = (home * RD + tile_row).astype(jnp.int32)
    nbr = tile_nbr.astype(jnp.int32)
    local = nbr < RD
    below = (nbr >= RD) & (nbr < RD + HALO)
    above = nbr >= RD + HALO
    src_below = (jnp.maximum(slab - 1, 0) * N_WIDE + dest).astype(jnp.int32)
    src_above = (jnp.minimum(slab + 1, N_SLAB - 1) * N_WIDE + dest).astype(jnp.int32)
    row_below = halo_list[src_below, 0, jnp.clip(nbr - RD, 0, HALO - 1)]
    row_above = halo_list[src_above, 1, jnp.clip(nbr - RD - HALO, 0, HALO - 1)]
    glob = jnp.where(local, home * RD + nbr, jnp.where(below, src_below * RD + row_below, src_above * RD + row_above)).astype(jnp.int32)
    live = local | below & (slab > 0) | above & (slab < N_SLAB - 1)
    rows_all = devices * RD

    def product(vec):
        vb = vec.astype(jnp.bfloat16)
        v_own = vb[own].reshape(devices, FT, width, tile)
        v_nbr = jnp.where(live[:, None, None], vb[glob], jnp.zeros((), vb.dtype)).reshape(devices, FT, width, tile)

        def contrib(item):
            blk, first, second = item
            blk_f = blk.astype(jnp.float32)
            part = jnp.einsum('tijc,tjc->tic', blk_f[:, 0], first.astype(jnp.float32))
            return part + jnp.einsum('tijc,tjc->tic', blk_f[:, 1], second.astype(jnp.float32))
        terms = lax.map(contrib, (blocks, v_own, v_nbr)).reshape(devices * FT, width, tile)
        faces = jax.ops.segment_sum(terms, own, num_segments=rows_all)
        return faces + source_product(vb, cell_state, cell_tau, cell_rate, species_weight)
    first_product = product(newton_residual)
    second_product = product(first_product)
    return (first_product, second_product)
```

```python
import functools

import jax
import jax.numpy as jnp
from jax import lax
from jax.experimental import pallas as pl
from jax.experimental.pallas import tpu as pltpu
from jax.sharding import PartitionSpec as P

CAP = 4
MESH = pl.DeviceIdType.MESH
F32 = jnp.float32
BF16 = jnp.bfloat16


def each(low, high, body):
    if high - low <= 8:
        for i in range(low, high):
            body(i)
    else:

        def step(i, carry):
            body(i)
            return carry

        lax.fori_loop(low, high, step, 0)


def kernel(
    owners,
    slabs,
    fo_hbm,
    fn_hbm,
    lin_hbm,
    quad_hbm,
    weight_hbm,
    state_hbm,
    tau_hbm,
    rate_hbm,
    res_hbm,
    dest_hbm,
    row_hbm,
    nbr_hbm,
    halo_hbm,
    outv1,
    outv2,
    fo,
    fn,
    lin,
    quad,
    state,
    tau,
    rate,
    res,
    faces,
    got,
    uf,
    speed,
    meta,
    got_meta,
    flux,
    flin,
    coef,
    acc,
    vown1,
    vown2,
    ext1,
    ext2,
    stage1,
    stage2,
    in_sem,
    face_send,
    face_recv,
    meta_send,
    meta_recv,
    halo_send,
    halo_recv,
    ready,
    halo_ready,
    weight_ref,
    dest_ref,
    row_ref,
    nbr_ref,
    halo_ref,
):
    s = lax.axis_index("slab")
    w = lax.axis_index("wide")
    count, width, tile = fo.shape
    rows = res.shape[0]
    nspec = weight_ref.shape[0]
    halo = halo_ref.shape[2]

    barrier = pltpu.get_barrier_semaphore()
    even = lax.rem(s, 2) == 0
    has_down = s > 0
    has_up = s < slabs - 1

    loads = []
    for i, (a, b) in enumerate(
        (
            (dest_hbm, dest_ref),
            (row_hbm, row_ref),
            (nbr_hbm, nbr_ref),
            (fo_hbm, fo),
            (fn_hbm, fn),
            (halo_hbm, halo_ref),
            (res_hbm, res),
            (quad_hbm, quad),
            (lin_hbm, lin),
            (state_hbm, state),
            (tau_hbm, tau),
            (rate_hbm, rate),
            (weight_hbm, weight_ref),
        )
    ):
        copy = pltpu.make_async_copy(a, b, in_sem.at[i])
        copy.start()
        loads.append(copy)

    def signal(sem, slab, wide):
        pl.semaphore_signal(sem, inc=1, device_id=(slab, wide), device_id_type=MESH)

    def greet(off):
        @pl.when(w + off < owners)
        def _():
            signal(barrier, s, w + off)

    each(1, owners, greet)

    @pl.when(jnp.logical_not(even))
    def _():
        signal(barrier, s - 1, w)

        @pl.when(has_up)
        def _():
            signal(barrier, s + 1, w)

    around = jnp.where(has_down, 1, 0) + jnp.where(has_up, 1, 0)
    greeted = w + jnp.where(even, around, 0)

    @pl.when(greeted > 0)
    def _():
        pl.semaphore_wait(barrier, greeted)


    def answer(off):
        @pl.when(w - off >= 0)
        def _():
            signal(ready.at[w], s, w - off)

    each(1, owners, answer)

    @pl.when(even)
    def _():
        @pl.when(has_down)
        def _():
            signal(halo_ready.at[1], s - 1, w)

        @pl.when(has_up)
        def _():
            signal(halo_ready.at[0], s + 1, w)

    bits = count.bit_length()
    mask = (1 << bits) - 1

    def picks(peer):
        packed = jnp.int32(0)
        for t in range(count):
            packed = jnp.where(dest_ref[t] == peer, packed * (1 << bits) + (t + 1), packed)
        return [(packed >> (bits * c)) & mask for c in range(CAP)]

    def fill(d, own):
        found = picks(d)
        for c in range(CAP):
            source = jnp.maximum(found[c] - 1, 0)
            row = jnp.where(found[c] > 0, row_ref[source], rows)
            nbr = jnp.where(found[c] > 0, nbr_ref[source], 0)
            if own:
                got_meta[w, c] = row
                got_meta[w, CAP + c] = nbr
                got[w, c, 0] = fo[source]
                got[w, c, 1] = fn[source]
            else:
                meta[d, c] = row
                meta[d, CAP + c] = nbr
                faces[d, c, 0] = fo[source]
                faces[d, c, 1] = fn[source]

    def face_copy(src, dst, peer):
        return pltpu.make_async_remote_copy(
            src_ref=faces.at[src],
            dst_ref=got.at[dst],
            send_sem=face_send.at[src],
            recv_sem=face_recv.at[dst],
            device_id=(s, peer),
            device_id_type=MESH,
        )

    def meta_copy(src, dst, peer):
        return pltpu.make_async_remote_copy(
            src_ref=meta.at[src],
            dst_ref=got_meta.at[dst],
            send_sem=meta_send.at[src],
            recv_sem=meta_recv.at[dst],
            device_id=(s, peer),
            device_id_type=MESH,
        )

    def send(peer):
        meta_copy(peer, w, peer).start()
        face_copy(peer, w, peer).start()

    for load in loads[:5]:
        load.wait()

    def send_lower(i):
        peer = w - (owners - i)

        @pl.when(peer >= 0)
        def _():
            fill(peer, False)
            send(peer)

    each(1, owners, send_lower)

    def up_copy(phase, stage, ext):
        return pltpu.make_async_remote_copy(
            src_ref=stage.at[0],
            dst_ref=ext.at[pl.ds(rows, halo)],
            send_sem=halo_send.at[phase, 0],
            recv_sem=halo_recv.at[phase, 0],
            device_id=(s + 1, w),
            device_id_type=MESH,
        )

    def down_copy(phase, stage, ext):
        return pltpu.make_async_remote_copy(
            src_ref=stage.at[1],
            dst_ref=ext.at[pl.ds(rows + halo, halo)],
            send_sem=halo_send.at[phase, 1],
            recv_sem=halo_recv.at[phase, 1],
            device_id=(s - 1, w),
            device_id_type=MESH,
        )

    def send_up(phase, stage, ext):
        @pl.when(has_up)
        def _():
            up_copy(phase, stage, ext).start()

    def send_down(phase, stage, ext):
        @pl.when(has_down)
        def _():
            down_copy(phase, stage, ext).start()

    def wait_halo(phase, stage, ext):
        @pl.when(has_down)
        def _():
            up_copy(phase, stage, ext).wait_recv()

        @pl.when(has_up)
        def _():
            down_copy(phase, stage, ext).wait_recv()

    def stage_halo(vown, stage):
        for h in range(halo):
            stage[0, h] = vown[halo_ref[0, 0, h]]
            stage[1, h] = vown[halo_ref[0, 1, h]]

    loads[5].wait()
    loads[6].wait()

    def round_rows(r, carry):
        vb = res[r].astype(BF16)
        vown1[r] = vb
        ext1[r] = vb
        return carry

    lax.fori_loop(0, rows, round_rows, 0, unroll=4)
    stage_halo(vown1, stage1)

    @pl.when(even)
    def _():
        send_up(0, stage1, ext1)
        send_down(0, stage1, ext1)

    for ext in (ext1, ext2):

        @pl.when(s == 0)
        def _():
            ext[pl.ds(rows, halo)] = jnp.zeros((halo, width, tile), BF16)

        @pl.when(s == slabs - 1)
        def _():
            ext[pl.ds(rows + halo, halo)] = jnp.zeros((halo, width, tile), BF16)

    def fill_higher(off):
        @pl.when(w + off < owners)
        def _():
            fill(w + off, False)

    each(1, owners, fill_higher)
    fill(w, True)

    def send_higher(off):
        peer = w + off

        @pl.when(peer < owners)
        def _():
            pl.semaphore_wait(ready.at[peer], 1)
            send(peer)

    send_higher(1)

    loads[7].wait()
    loads[8].wait()
    wide = width * width
    fq = quad[...].astype(F32) * 0.5
    own_lane = lax.broadcasted_iota(jnp.int32, (width, wide), 1) // width
    own_sub = lax.broadcasted_iota(jnp.int32, (width, wide), 0)
    keep = own_lane == own_sub
    lane_block = lax.broadcasted_iota(jnp.int32, (width, tile), 1) // width
    per = tile // width
    for half in range(wide // tile):
        total = jnp.zeros((width, tile), F32)
        for m in range(per):
            k = half * per + m
            spread = jnp.where(keep, jnp.broadcast_to(fq[k : k + 1, :], (width, wide)), 0.0)
            fold = spread[:, :tile]
            for piece in range(1, wide // tile):
                fold = fold + spread[:, piece * tile : (piece + 1) * tile]
            step = tile // 2
            while step >= width:
                fold = fold + pltpu.roll(fold, step, 1)
                step //= 2
            total = jnp.where(lane_block == m, fold, total)
        flux[:, half * tile : (half + 1) * tile] = total.astype(BF16)
    half_lin = lin[...] * 0.5
    high = half_lin.astype(BF16)
    flin[:, :width] = high
    flin[:, width:] = (half_lin - high.astype(F32)).astype(BF16)

    @pl.when(jnp.logical_not(even))
    def _():
        pl.semaphore_wait(halo_ready.at[0], 1)
        send_down(0, stage1, ext1)

        @pl.when(has_up)
        def _():
            pl.semaphore_wait(halo_ready.at[1], 1)
            send_up(0, stage1, ext1)

    for load in loads[9:]:
        load.wait()
    sub = lax.broadcasted_iota(jnp.int32, (width, tile), 0)
    relax = jnp.where(sub == 14, 1.0, 0.0) - jnp.where(sub == 15, 1.0, 0.0)
    mixture = jnp.zeros((width, tile), F32)
    for m in range(nspec):
        mixture = jnp.where(sub == m, weight_ref[m], mixture)

    def prepare(r, carry):
        u = state[r].astype(F32)
        inv = 1.0 / tau[pl.ds(r, 1), :]
        rho = jnp.sum(mixture * u, axis=0, keepdims=True) * inv
        gap = jnp.sum(relax * u, axis=0, keepdims=True) * inv
        coef[r] = gap * mixture + rho * relax
        return carry

    lax.fori_loop(0, rows, prepare, 0, unroll=4)

    def diagonal(vown):
        def one(r, carry):
            v = vown[r].astype(F32)
            change = jnp.sum(coef[r] * v, axis=0, keepdims=True)
            acc[r] = rate[pl.ds(r, 1), :] * v + relax * change
            return carry

        lax.fori_loop(0, rows, one, 0, unroll=4)

    diagonal(vown1)

    each(2, owners, send_higher)

    def side(q, which, vectors):
        blocks = []
        for c in range(CAP):
            v = vectors[c]
            blocks.append(
                jnp.concatenate(
                    [
                        jnp.broadcast_to(uf[q, c, which, pl.ds(k, 1), :], (width, tile)).astype(BF16) * v
                        for k in range(width)
                    ],
                    axis=0,
                )
            )
        outer = jnp.concatenate(blocks, axis=1)
        plain = jnp.concatenate([jnp.concatenate([v, v], axis=0) for v in vectors], axis=1)
        return jnp.dot(flux[...], outer, preferred_element_type=F32) + jnp.dot(
            flin[...], plain, preferred_element_type=F32
        )

    def own_side(q, vown):
        vectors = [vown[jnp.minimum(got_meta[q, c], rows - 1)] for c in range(CAP)]
        out = side(q, 0, vectors)
        return [
            out[:, c * tile : (c + 1) * tile] + speed[q, pl.ds(c, 1), :] * vectors[c].astype(F32)
            for c in range(CAP)
        ]

    def nbr_side(q, ext):
        vectors = [ext[got_meta[q, CAP + c]] for c in range(CAP)]
        out = side(q, 1, vectors)
        return [
            out[:, c * tile : (c + 1) * tile] - speed[q, pl.ds(c, 1), :] * vectors[c].astype(F32)
            for c in range(CAP)
        ]

    def add_rows(q, terms):
        for r in range(rows):
            total = acc[r]
            for c in range(CAP):
                total = total + jnp.where(got_meta[q, c] == r, terms[c], 0.0)
            acc[r] = total

    def unpack(q):
        for c in range(CAP):
            own = got[q, c, 0].astype(F32)
            nbr = got[q, c, 1].astype(F32)
            uf[q, c, 0] = own
            uf[q, c, 1] = nbr
            square = jnp.sum(own * own + nbr * nbr, axis=0, keepdims=True)
            speed[q, pl.ds(c, 1), :] = 0.5 + 0.5 * jnp.sqrt(square * (0.5 / width))

    wait_halo(0, stage1, ext1)
    near = jnp.minimum(w, owners - 1 - w)

    def first_part(off, carry):
        apart = jnp.where(off <= 2 * near, (off + 1) // 2, off - near)
        below = jnp.where(off <= 2 * near, lax.rem(off, 2) == 1, 2 * w >= owners)
        q = jnp.where(below, w - apart, w + apart)

        @pl.when(off > 0)
        def _():
            meta_copy(q, q, q).wait_recv()
            face_copy(q, q, q).wait_recv()

        unpack(q)
        a = own_side(q, vown1)
        b = nbr_side(q, ext1)
        add_rows(q, [a[c] + b[c] for c in range(CAP)])
        return carry

    lax.fori_loop(0, owners, first_part, 0)

    for r in range(rows):
        value = acc[r]
        outv1[r] = value
        vb = value.astype(BF16)
        vown2[r] = vb
        ext2[r] = vb
    stage_halo(vown2, stage2)
    send_up(1, stage2, ext2)
    send_down(1, stage2, ext2)

    diagonal(vown2)

    def second_own(q, carry):
        add_rows(q, own_side(q, vown2))
        return carry

    lax.fori_loop(0, owners, second_own, 0, unroll=4)
    wait_halo(1, stage2, ext2)

    def second_nbr(q, carry):
        add_rows(q, nbr_side(q, ext2))
        return carry

    lax.fori_loop(0, owners, second_nbr, 0, unroll=4)
    for r in range(rows):
        outv2[r] = acc[r]

    def sent(off):
        for peer in (w + off, w - off):

            @pl.when((peer >= 0) & (peer < owners))
            def _():
                meta_copy(peer, w, peer).wait_send()
                face_copy(peer, w, peer).wait_send()

    each(1, owners, sent)
    for phase, stage, ext in ((0, stage1, ext1), (1, stage2, ext2)):

        @pl.when(has_up)
        def _():
            up_copy(phase, stage, ext).wait_send()

        @pl.when(has_down)
        def _():
            down_copy(phase, stage, ext).wait_send()


def store(a, b, c, d, sem):
    first = pltpu.make_async_copy(a, c, sem.at[0])
    second = pltpu.make_async_copy(b, d, sem.at[1])
    first.start()
    second.start()
    first.wait()
    second.wait()


def solution(mesh):
    owners = mesh.shape["wide"]
    slabs = mesh.shape["slab"]

    def on_device(fo, fn, lin, quad, weight, state, tau, rate, res, dest, row, nbr, halo_list):
        count, width, tile = fo.shape
        rows = res.shape[0]
        halo = halo_list.shape[2]
        hbm = pl.BlockSpec(memory_space=pltpu.MemorySpace.HBM)
        vmem = pl.BlockSpec(memory_space=pltpu.MemorySpace.VMEM)
        dma = pltpu.SemaphoreType.DMA
        row_set = (rows, width, tile)
        products = pl.pallas_call(
            functools.partial(kernel, owners, slabs),
            out_shape=(pltpu.VMEM(row_set, F32), pltpu.VMEM(row_set, F32)),
            in_specs=[hbm] * 13,
            out_specs=(vmem, vmem),
            scratch_shapes=[
                pltpu.VMEM(fo.shape, BF16),
                pltpu.VMEM(fn.shape, BF16),
                pltpu.VMEM(lin.shape, F32),
                pltpu.VMEM(quad.shape, BF16),
                pltpu.VMEM(state.shape, BF16),
                pltpu.VMEM(tau.shape, F32),
                pltpu.VMEM(rate.shape, F32),
                pltpu.VMEM(row_set, F32),
                pltpu.VMEM((owners, CAP, 2, width, tile), BF16),
                pltpu.VMEM((owners, CAP, 2, width, tile), BF16),
                pltpu.VMEM((owners, CAP, 2, width, tile), F32),
                pltpu.VMEM((owners, 8, tile), F32),
                pltpu.SMEM((owners, 2 * CAP), jnp.int32),
                pltpu.SMEM((owners, 2 * CAP), jnp.int32),
                pltpu.VMEM((width, width * width), BF16),
                pltpu.VMEM((width, 2 * width), BF16),
                pltpu.VMEM(row_set, F32),
                pltpu.VMEM(row_set, F32),
                pltpu.VMEM(row_set, BF16),
                pltpu.VMEM(row_set, BF16),
                pltpu.VMEM((rows + 2 * halo, width, tile), BF16),
                pltpu.VMEM((rows + 2 * halo, width, tile), BF16),
                pltpu.VMEM((2, halo, width, tile), BF16),
                pltpu.VMEM((2, halo, width, tile), BF16),
                dma((13,)),
                dma((owners,)),
                dma((owners,)),
                dma((owners,)),
                dma((owners,)),
                dma((2, 2)),
                dma((2, 2)),
                pltpu.SemaphoreType.REGULAR((owners,)),
                pltpu.SemaphoreType.REGULAR((2,)),
                pltpu.SMEM(weight.shape, F32),
                pltpu.SMEM((count,), jnp.int32),
                pltpu.SMEM(row.shape, jnp.int32),
                pltpu.SMEM(nbr.shape, jnp.int32),
                pltpu.SMEM(halo_list.shape, jnp.int32),
            ],
            compiler_params=pltpu.CompilerParams(collective_id=0, has_side_effects=True),
        )(fo, fn, lin, quad, weight, state, tau, rate, res, dest.reshape(count), row, nbr, halo_list)
        return pl.pallas_call(
            store,
            out_shape=(jax.ShapeDtypeStruct(row_set, F32), jax.ShapeDtypeStruct(row_set, F32)),
            in_specs=[vmem, vmem],
            out_specs=(hbm, hbm),
            scratch_shapes=[dma((2,))],
        )(*[pltpu.with_memory_space_constraint(x, pltpu.MemorySpace.VMEM) for x in products])

    every = ("slab", "wide")
    cube, flat = P(every, None, None), P(every, None)
    return jax.shard_map(
        on_device,
        mesh=mesh,
        in_specs=(cube, cube, P(), P(), P(), cube, flat, flat, cube, flat, P(every), P(every), cube),
        out_specs=(cube, cube),
        check_vma=False,
    )
```

```python
import functools

import jax
import jax.numpy as jnp
from jax import lax
from jax.experimental import pallas as pl
from jax.experimental.pallas import tpu as pltpu
from jax.sharding import PartitionSpec as P

CAP = 4
MESH = pl.DeviceIdType.MESH
F32 = jnp.float32
BF16 = jnp.bfloat16


def each(low, high, body):
    if high - low <= 8:
        for i in range(low, high):
            body(i)
    else:

        def step(i, carry):
            body(i)
            return carry

        lax.fori_loop(low, high, step, 0)


def kernel(
    owners,
    slabs,
    fo_hbm,
    fn_hbm,
    lin_hbm,
    quad_hbm,
    weight_hbm,
    state_hbm,
    tau_hbm,
    rate_hbm,
    res_hbm,
    dest_hbm,
    row_hbm,
    nbr_hbm,
    halo_hbm,
    outv1,
    outv2,
    fo,
    fn,
    lin,
    quad,
    state,
    tau,
    rate,
    res,
    faces,
    got,
    speed,
    meta,
    got_meta,
    flux,
    mats,
    coef,
    acc,
    part,
    vf1,
    vf2,
    stage,
    land,
    face_send,
    face_recv,
    meta_send,
    meta_recv,
    halo_send,
    halo_recv,
    ready,
    halo_ready,
    weight_ref,
    dest_ref,
    row_ref,
    nbr_ref,
    halo_ref,
    latest,
    before,
    own_row,
    nbr_row,
):
    s = lax.axis_index("slab")
    w = lax.axis_index("wide")
    count, width, tile = fo.shape
    rows = res.shape[0]
    nspec = weight_ref.shape[0]
    halo = halo_ref.shape[2]
    wide = width * width
    first_slot = rows + 1

    barrier = pltpu.get_barrier_semaphore()
    even = lax.rem(s, 2) == 0
    has_down = s > 0
    has_up = s < slabs - 1
    inner = has_down & has_up

    def signal(sem, slab, wide):
        pl.semaphore_signal(sem, inc=1, device_id=(slab, wide), device_id_type=MESH)

    def greet(off):
        @pl.when(w + off < owners)
        def _():
            signal(barrier, s, w + off)

    def answer(off):
        @pl.when(w - off >= 0)
        def _():
            signal(ready.at[w - 1], s, w - off)

    bits = count.bit_length()
    mask = (1 << bits) - 1

    def picks(peer):
        packed = jnp.int32(0)
        for t in range(count):
            packed = jnp.where(dest_ref[t] == peer, packed * (1 << bits) + (t + 1), packed)
        return [(packed >> (bits * c)) & mask for c in range(CAP)]

    def fill(d, own):
        found = picks(d)
        for c in range(CAP):
            source = jnp.maximum(found[c] - 1, 0)
            row = jnp.where(found[c] > 0, row_ref[source], rows)
            nbr = jnp.where(found[c] > 0, nbr_ref[source], 0)
            if own:
                got_meta[w, c] = row
                got_meta[w, CAP + c] = nbr
                got[w, c, 0] = fo[source]
                got[w, c, 1] = fn[source]
            else:
                meta[d, c] = row
                meta[d, CAP + c] = nbr
                faces[d, c, 0] = fo[source]
                faces[d, c, 1] = fn[source]

    def order(peer):
        return peer - jnp.where(peer > w, 1, 0)

    def face_copy(peer):
        return pltpu.make_async_remote_copy(
            src_ref=faces.at[peer],
            dst_ref=got.at[w],
            send_sem=face_send,
            recv_sem=face_recv.at[w - jnp.where(w > peer, 1, 0)],
            device_id=(s, peer),
            device_id_type=MESH,
        )

    def meta_copy(peer):
        return pltpu.make_async_remote_copy(
            src_ref=meta.at[peer],
            dst_ref=got_meta.at[w],
            send_sem=meta_send,
            recv_sem=meta_recv.at[w - jnp.where(w > peer, 1, 0)],
            device_id=(s, peer),
            device_id_type=MESH,
        )

    def send(peer):
        meta_copy(peer).start()
        face_copy(peer).start()

    def send_lower(i):
        peer = w - (owners - i)

        @pl.when(peer >= 0)
        def _():
            fill(peer, False)
            send(peer)

    def fill_higher(off):
        @pl.when(w + off < owners)
        def _():
            fill(w + off, False)

    def send_higher(off):
        peer = w + off

        @pl.when(peer < owners)
        def _():
            pl.semaphore_wait(ready.at[peer - 1], 1)
            send(peer)

    def up_copy(phase):
        return pltpu.make_async_remote_copy(
            src_ref=stage.at[phase, 0],
            dst_ref=land.at[phase, 0],
            send_sem=halo_send,
            recv_sem=halo_recv.at[phase],
            device_id=(s + 1, w),
            device_id_type=MESH,
        )

    def down_copy(phase):
        return pltpu.make_async_remote_copy(
            src_ref=stage.at[phase, 1],
            dst_ref=land.at[phase, 1],
            send_sem=halo_send,
            recv_sem=halo_recv.at[phase],
            device_id=(s - 1, w),
            device_id_type=MESH,
        )

    def send_halo(phase):
        @pl.when(has_up)
        def _():
            up_copy(phase).start()

        @pl.when(has_down)
        def _():
            down_copy(phase).start()

    def settle(sem, many, few):
        @pl.when(inner)
        def _():
            pltpu.make_async_copy(many, many, sem).wait()

        @pl.when(jnp.logical_not(inner))
        def _():
            pltpu.make_async_copy(few, few, sem).wait()

    def take_halo(phase, vf):
        settle(halo_recv.at[phase], land.at[phase], land.at[phase, 0])

        @pl.when(has_down)
        def _():
            for h in range(halo):
                vf[rows + h] = land[phase, 0, h].astype(F32)

        @pl.when(has_up)
        def _():
            for h in range(halo):
                vf[rows + halo + h] = land[phase, 1, h].astype(F32)

    def link(off, q):
        named = [got_meta[q, c] for c in range(CAP)]
        at = first_slot + off * CAP
        for c in range(CAP):
            last = latest[named[c]]
            for e in range(c):
                last = jnp.where(named[e] == named[c], at + e, last)
            before[off * CAP + c] = last
            own_row[off * CAP + c] = jnp.minimum(named[c], rows - 1)
            nbr_row[off * CAP + c] = got_meta[q, CAP + c]
        for r in range(rows):
            last = latest[r]
            for c in range(CAP):
                last = jnp.where(named[c] == r, at + c, last)
            latest[r] = last

    def assemble(off, q):
        for c in range(CAP):
            own = got[q, c, 0].astype(F32)
            nbr = got[q, c, 1].astype(F32)
            square = jnp.sum(own * own + nbr * nbr, axis=0, keepdims=True)
            speed[off, pl.ds(c, 1), :] = 0.5 + 0.5 * jnp.sqrt(square * (0.5 / width))
        for c in range(CAP):
            states = jnp.concatenate([got[q, c, 0], got[q, c, 1]], axis=1)
            ones = jnp.ones((2 * width, 2 * tile), BF16)
            both = jnp.dot(flux[...], jnp.concatenate([states, ones], axis=0), preferred_element_type=F32)
            mats[off, c, 0] = both[:, :tile]
            mats[off, c, 1] = both[:, tile:]

    def times(off, c, side, vf, row, total):
        for j in range(width):
            block = mats[off, c, side, j * width : (j + 1) * width, :]
            total = total + block * jnp.broadcast_to(vf[row, pl.ds(j, 1), :], (width, tile))
        return total

    def owned(off, c, vf):
        row = own_row[off * CAP + c]
        return times(off, c, 0, vf, row, speed[off, pl.ds(c, 1), :] * vf[row])

    def neighboured(off, c, vf):
        row = nbr_row[off * CAP + c]
        return times(off, c, 1, vf, row, -speed[off, pl.ds(c, 1), :] * vf[row])

    def chain(off, c, term):
        acc[first_slot + off * CAP + c] = term + acc[before[off * CAP + c]]

    def run(in_sem):
        loads = [
            pltpu.make_async_copy(a, b, in_sem.at[i])
            for i, (a, b) in enumerate(
                (
                    (dest_hbm, dest_ref),
                    (row_hbm, row_ref),
                    (nbr_hbm, nbr_ref),
                    (fo_hbm, fo),
                    (fn_hbm, fn),
                    (halo_hbm, halo_ref),
                    (res_hbm, res),
                    (quad_hbm, quad),
                    (lin_hbm, lin),
                    (state_hbm, state),
                    (tau_hbm, tau),
                    (rate_hbm, rate),
                    (weight_hbm, weight_ref),
                )
            )
        ]
        for load in loads[:5]:
            load.start()
        each(1, owners, greet)

        @pl.when(jnp.logical_not(even))
        def _():
            signal(barrier, s - 1, w)

            @pl.when(has_up)
            def _():
                signal(barrier, s + 1, w)

        for load in loads[5:]:
            load.start()
        around = jnp.where(has_down, 1, 0) + jnp.where(has_up, 1, 0)
        greeted = w + jnp.where(even, around, 0)

        @pl.when(greeted > 0)
        def _():
            pl.semaphore_wait(barrier, greeted)

        each(1, owners, answer)

        @pl.when(even)
        def _():
            @pl.when(has_down)
            def _():
                signal(halo_ready.at[1], s - 1, w)

            @pl.when(has_up)
            def _():
                signal(halo_ready.at[0], s + 1, w)

        for load in loads[:5]:
            load.wait()
        each(1, owners, send_lower)
        loads[5].wait()
        loads[6].wait()

        def round_rows(r, carry):
            vf1[r] = res[r].astype(BF16).astype(F32)
            return carry

        lax.fori_loop(0, rows, round_rows, 0, unroll=4)
        for h in range(halo):
            stage[0, 0, h] = vf1[halo_ref[0, 0, h]].astype(BF16)
            stage[0, 1, h] = vf1[halo_ref[0, 1, h]].astype(BF16)

        @pl.when(even)
        def _():
            send_halo(0)

        each(1, owners, fill_higher)
        fill(w, True)
        send_higher(1)

        for r in range(rows + 1):
            latest[r] = r
        acc[rows] = jnp.zeros((width, tile), F32)
        for vf in (vf1, vf2):

            @pl.when(s == 0)
            def _():
                vf[pl.ds(rows, halo)] = jnp.zeros((halo, width, tile), F32)

            @pl.when(s == slabs - 1)
            def _():
                vf[pl.ds(rows + halo, halo)] = jnp.zeros((halo, width, tile), F32)

        loads[7].wait()
        loads[8].wait()
        at = lax.broadcasted_iota(jnp.int32, (wide, wide), 0)
        column = lax.broadcasted_iota(jnp.int32, (wide, wide), 1)
        swap = jnp.where(column == lax.rem(at, width) * width + at // width, 1.0, 0.0).astype(BF16)
        flux[:, :width] = (
            lax.dot_general(swap, quad[...], (((1,), (1,)), ((), ())), preferred_element_type=F32) * 0.5
        ).astype(BF16)
        half_lin = lin[...] * 0.5
        high = half_lin.astype(BF16)
        low = (half_lin - high.astype(F32)).astype(BF16)
        at = lax.broadcasted_iota(jnp.int32, (wide, width), 0)
        column = lax.broadcasted_iota(jnp.int32, (wide, width), 1)
        pick = jnp.where(column == lax.rem(at, width), 1.0, 0.0).astype(BF16)
        keep = column == at // width
        for i, term in enumerate((high, low)):
            flux[:, (1 + i) * width : (2 + i) * width] = jnp.where(
                keep, jnp.dot(pick, term, preferred_element_type=F32), 0.0
            ).astype(BF16)

        @pl.when(jnp.logical_not(even))
        def _():
            pl.semaphore_wait(halo_ready.at[0], 1)
            down_copy(0).start()

            @pl.when(has_up)
            def _():
                pl.semaphore_wait(halo_ready.at[1], 1)
                up_copy(0).start()

        for load in loads[9:]:
            load.wait()

    pl.run_scoped(run, pltpu.SemaphoreType.DMA((13,)))

    sub = lax.broadcasted_iota(jnp.int32, (width, tile), 0)
    relax = jnp.where(sub == 14, 1.0, 0.0) - jnp.where(sub == 15, 1.0, 0.0)
    mixture = jnp.zeros((width, tile), F32)
    for m in range(nspec):
        mixture = jnp.where(sub == m, weight_ref[m], mixture)

    def prepare(r, carry):
        u = state[r].astype(F32)
        inv = 1.0 / tau[pl.ds(r, 1), :]
        rho = jnp.sum(mixture * u, axis=0, keepdims=True) * inv
        gap = jnp.sum(relax * u, axis=0, keepdims=True) * inv
        coef[r] = gap * mixture + rho * relax
        return carry

    lax.fori_loop(0, rows, prepare, 0, unroll=4)

    def diagonal(vf):
        def one(r, carry):
            v = vf[r]
            change = jnp.sum(coef[r] * v, axis=0, keepdims=True)
            acc[r] = rate[pl.ds(r, 1), :] * v + relax * change
            return carry

        lax.fori_loop(0, rows, one, 0, unroll=4)

    diagonal(vf1)
    each(2, owners, send_higher)
    take_halo(0, vf1)
    near = jnp.minimum(w, owners - 1 - w)

    def first_part(off, carry):
        apart = jnp.where(off <= 2 * near, (off + 1) // 2, off - near)
        below = jnp.where(off <= 2 * near, lax.rem(off, 2) == 1, 2 * w >= owners)
        q = jnp.where(below, w - apart, w + apart)

        @pl.when(off > 0)
        def _():
            pltpu.make_async_copy(got_meta.at[q], got_meta.at[q], meta_recv.at[order(q)]).wait()

        link(off, q)

        @pl.when(off > 0)
        def _():
            pltpu.make_async_copy(got.at[q], got.at[q], face_recv.at[order(q)]).wait()

        assemble(off, q)
        for c in range(CAP):
            chain(off, c, owned(off, c, vf1) + neighboured(off, c, vf1))
        return carry

    lax.fori_loop(0, owners, first_part, 0)

    for h in range(halo):
        stage[1, 0, h] = acc[latest[halo_ref[0, 0, h]]].astype(BF16)
        stage[1, 1, h] = acc[latest[halo_ref[0, 1, h]]].astype(BF16)
    send_halo(1)
    for r in range(rows):
        value = acc[latest[r]]
        outv1[r] = value
        vf2[r] = value.astype(BF16).astype(F32)
    diagonal(vf2)

    def second_own(off, carry):
        for c in range(CAP):
            part[off * CAP + c] = owned(off, c, vf2)
        return carry

    lax.fori_loop(0, owners, second_own, 0)
    pltpu.make_async_copy(faces.at[pl.ds(0, owners - 1)], faces.at[pl.ds(0, owners - 1)], face_send).wait()
    pltpu.make_async_copy(meta.at[pl.ds(0, owners - 1)], meta.at[pl.ds(0, owners - 1)], meta_send).wait()
    take_halo(1, vf2)

    def second_nbr(off, carry):
        for c in range(CAP):
            chain(off, c, part[off * CAP + c] + neighboured(off, c, vf2))
        return carry

    lax.fori_loop(0, owners, second_nbr, 0, unroll=4)
    for r in range(rows):
        outv2[r] = acc[latest[r]]
    settle(halo_send, stage, stage.at[0])


def store(a, b, c, d, sem):
    first = pltpu.make_async_copy(a, c, sem.at[0])
    second = pltpu.make_async_copy(b, d, sem.at[1])
    first.start()
    second.start()
    first.wait()
    second.wait()


def solution(mesh):
    owners = mesh.shape["wide"]
    slabs = mesh.shape["slab"]

    def on_device(fo, fn, lin, quad, weight, state, tau, rate, res, dest, row, nbr, halo_list):
        count, width, tile = fo.shape
        rows = res.shape[0]
        halo = halo_list.shape[2]
        hbm = pl.BlockSpec(memory_space=pltpu.MemorySpace.HBM)
        vmem = pl.BlockSpec(memory_space=pltpu.MemorySpace.VMEM)
        dma = pltpu.SemaphoreType.DMA
        row_set = (rows, width, tile)
        products = pl.pallas_call(
            functools.partial(kernel, owners, slabs),
            out_shape=(pltpu.VMEM(row_set, F32), pltpu.VMEM(row_set, F32)),
            in_specs=[hbm] * 13,
            out_specs=(vmem, vmem),
            scratch_shapes=[
                pltpu.VMEM(fo.shape, BF16),
                pltpu.VMEM(fn.shape, BF16),
                pltpu.VMEM(lin.shape, F32),
                pltpu.VMEM(quad.shape, BF16),
                pltpu.VMEM(state.shape, BF16),
                pltpu.VMEM(tau.shape, F32),
                pltpu.VMEM(rate.shape, F32),
                pltpu.VMEM(row_set, F32),
                pltpu.VMEM((owners, CAP, 2, width, tile), BF16),
                pltpu.VMEM((owners, CAP, 2, width, tile), BF16),
                pltpu.VMEM((owners, 8, tile), F32),
                pltpu.SMEM((owners, 2 * CAP), jnp.int32),
                pltpu.SMEM((owners, 2 * CAP), jnp.int32),
                pltpu.VMEM((width * width, 3 * width), BF16),
                pltpu.VMEM((owners, CAP, 2, width * width, tile), F32),
                pltpu.VMEM(row_set, F32),
                pltpu.VMEM((rows + 1 + owners * CAP, width, tile), F32),
                pltpu.VMEM((owners * CAP, width, tile), F32),
                pltpu.VMEM((rows + 2 * halo, width, tile), F32),
                pltpu.VMEM((rows + 2 * halo, width, tile), F32),
                pltpu.VMEM((2, 2, halo, width, tile), BF16),
                pltpu.VMEM((2, 2, halo, width, tile), BF16),
                dma(()),
                dma((owners - 1,)),
                dma(()),
                dma((owners - 1,)),
                dma(()),
                dma((2,)),
                pltpu.SemaphoreType.REGULAR((owners - 1,)),
                pltpu.SemaphoreType.REGULAR((2,)),
                pltpu.SMEM(weight.shape, F32),
                pltpu.SMEM((count,), jnp.int32),
                pltpu.SMEM(row.shape, jnp.int32),
                pltpu.SMEM(nbr.shape, jnp.int32),
                pltpu.SMEM(halo_list.shape, jnp.int32),
                pltpu.SMEM((rows + 1,), jnp.int32),
                pltpu.SMEM((owners * CAP,), jnp.int32),
                pltpu.SMEM((owners * CAP,), jnp.int32),
                pltpu.SMEM((owners * CAP,), jnp.int32),
            ],
            compiler_params=pltpu.CompilerParams(collective_id=0, has_side_effects=True),
        )(fo, fn, lin, quad, weight, state, tau, rate, res, dest.reshape(count), row, nbr, halo_list)
        return pl.pallas_call(
            store,
            out_shape=(jax.ShapeDtypeStruct(row_set, F32), jax.ShapeDtypeStruct(row_set, F32)),
            in_specs=[vmem, vmem],
            out_specs=(hbm, hbm),
            scratch_shapes=[dma((2,))],
        )(*[pltpu.with_memory_space_constraint(x, pltpu.MemorySpace.VMEM) for x in products])

    every = ("slab", "wide")
    cube, flat = P(every, None, None), P(every, None)
    return jax.shard_map(
        on_device,
        mesh=mesh,
        in_specs=(cube, cube, P(), P(), P(), cube, flat, flat, cube, flat, P(every), P(every), cube),
        out_specs=(cube, cube),
        check_vma=False,
    )
```

```python
import functools

import jax
import jax.numpy as jnp
from jax import lax
from jax.experimental import pallas as pl
from jax.experimental.pallas import tpu as pltpu
from jax.sharding import PartitionSpec as P

CAP = 4
MESH = pl.DeviceIdType.MESH
F32 = jnp.float32
BF16 = jnp.bfloat16


def each(low, high, body):
    if high - low <= 8:
        for i in range(low, high):
            body(i)
    else:

        def step(i, carry):
            body(i)
            return carry

        lax.fori_loop(low, high, step, 0)


def kernel(
    owners,
    slabs,
    fo_hbm,
    fn_hbm,
    lin_hbm,
    quad_hbm,
    weight_hbm,
    state_hbm,
    tau_hbm,
    rate_hbm,
    res_hbm,
    dest_hbm,
    row_hbm,
    nbr_hbm,
    halo_hbm,
    outv1,
    outv2,
    fo,
    fn,
    lin,
    quad,
    state,
    tau,
    rate,
    res,
    faces,
    got,
    speed,
    meta,
    got_meta,
    uf,
    flux,
    form,
    bilinear,
    linear,
    flin,
    mats,
    coef,
    acc,
    part,
    vf1,
    vf2,
    stage,
    land,
    face_send,
    face_recv,
    meta_send,
    meta_recv,
    halo_send,
    halo_recv,
    ready,
    halo_ready,
    weight_ref,
    dest_ref,
    row_ref,
    nbr_ref,
    halo_ref,
    latest,
    before,
    own_row,
    nbr_row,
):
    s = lax.axis_index("slab")
    w = lax.axis_index("wide")
    count, width, tile = fo.shape
    rows = res.shape[0]
    nspec = weight_ref.shape[0]
    halo = halo_ref.shape[2]
    wide = width * width
    first_slot = rows + 1

    barrier = pltpu.get_barrier_semaphore()
    even = lax.rem(s, 2) == 0
    has_down = s > 0
    has_up = s < slabs - 1
    inner = has_down & has_up

    def signal(sem, slab, wide):
        pl.semaphore_signal(sem, inc=1, device_id=(slab, wide), device_id_type=MESH)

    def greet(off):
        @pl.when(w + off < owners)
        def _():
            signal(barrier, s, w + off)

    def answer(off):
        @pl.when(w - off >= 0)
        def _():
            signal(ready.at[w - 1], s, w - off)

    bits = count.bit_length()
    mask = (1 << bits) - 1

    def picks(peer):
        packed = jnp.int32(0)
        for t in range(count):
            packed = jnp.where(dest_ref[t] == peer, packed * (1 << bits) + (t + 1), packed)
        return [(packed >> (bits * c)) & mask for c in range(CAP)]

    def fill(d, own):
        found = picks(d)
        for c in range(CAP):
            source = jnp.maximum(found[c] - 1, 0)
            row = jnp.where(found[c] > 0, row_ref[source], rows)
            nbr = jnp.where(found[c] > 0, nbr_ref[source], 0)
            if own:
                got_meta[w, c] = row
                got_meta[w, CAP + c] = nbr
                got[w, c, 0] = fo[source]
                got[w, c, 1] = fn[source]
            else:
                meta[d, c] = row
                meta[d, CAP + c] = nbr
                faces[d, c, 0] = fo[source]
                faces[d, c, 1] = fn[source]

    def order(peer):
        return peer - jnp.where(peer > w, 1, 0)

    def face_copy(peer):
        return pltpu.make_async_remote_copy(
            src_ref=faces.at[peer],
            dst_ref=got.at[w],
            send_sem=face_send,
            recv_sem=face_recv.at[w - jnp.where(w > peer, 1, 0)],
            device_id=(s, peer),
            device_id_type=MESH,
        )

    def meta_copy(peer):
        return pltpu.make_async_remote_copy(
            src_ref=meta.at[peer],
            dst_ref=got_meta.at[w],
            send_sem=meta_send,
            recv_sem=meta_recv.at[w - jnp.where(w > peer, 1, 0)],
            device_id=(s, peer),
            device_id_type=MESH,
        )

    def send(peer):
        meta_copy(peer).start()
        face_copy(peer).start()

    def send_lower(i):
        peer = w - (owners - i)

        @pl.when(peer >= 0)
        def _():
            fill(peer, False)
            send(peer)

    def fill_higher(off):
        @pl.when(w + off < owners)
        def _():
            fill(w + off, False)

    def send_higher(off):
        peer = w + off

        @pl.when(peer < owners)
        def _():
            pl.semaphore_wait(ready.at[peer - 1], 1)
            send(peer)

    def up_copy(phase):
        return pltpu.make_async_remote_copy(
            src_ref=stage.at[phase, 0],
            dst_ref=land.at[phase, 0],
            send_sem=halo_send,
            recv_sem=halo_recv.at[phase],
            device_id=(s + 1, w),
            device_id_type=MESH,
        )

    def down_copy(phase):
        return pltpu.make_async_remote_copy(
            src_ref=stage.at[phase, 1],
            dst_ref=land.at[phase, 1],
            send_sem=halo_send,
            recv_sem=halo_recv.at[phase],
            device_id=(s - 1, w),
            device_id_type=MESH,
        )

    def send_halo(phase):
        @pl.when(has_down)
        def _():
            down_copy(phase).start()

        @pl.when(has_up)
        def _():
            up_copy(phase).start()

    def settle(sem, many, few):
        @pl.when(inner)
        def _():
            pltpu.make_async_copy(many, many, sem).wait()

        @pl.when(jnp.logical_not(inner))
        def _():
            pltpu.make_async_copy(few, few, sem).wait()

    def take_halo(phase, vf):
        settle(halo_recv.at[phase], land.at[phase], land.at[phase, 0])

        @pl.when(has_down)
        def _():
            for h in range(halo):
                vf[rows + h] = land[phase, 0, h].astype(F32)

        @pl.when(has_up)
        def _():
            for h in range(halo):
                vf[rows + halo + h] = land[phase, 1, h].astype(F32)

    def link(off, q):
        named = [got_meta[q, c] for c in range(CAP)]
        at = first_slot + off * CAP
        for c in range(CAP):
            last = latest[named[c]]
            for e in range(c):
                last = jnp.where(named[e] == named[c], at + e, last)
            before[off * CAP + c] = last
            own_row[off * CAP + c] = jnp.minimum(named[c], rows - 1)
            nbr_row[off * CAP + c] = got_meta[q, CAP + c]
        for r in range(rows):
            last = latest[r]
            for c in range(CAP):
                last = jnp.where(named[c] == r, at + c, last)
            latest[r] = last

    def unpack(off, q):
        for c in range(CAP):
            own = got[q, c, 0].astype(F32)
            nbr = got[q, c, 1].astype(F32)
            uf[off, c, 0] = own
            uf[off, c, 1] = nbr
            square = jnp.sum(own * own + nbr * nbr, axis=0, keepdims=True)
            speed[off, pl.ds(c, 1), :] = 0.5 + 0.5 * jnp.sqrt(square * (0.5 / width))

    def contract(low, high, vf):
        def pair(i, carry):
            at = low + 2 * i
            vectors = jnp.concatenate([vf[at].astype(BF16), vf[at + 1].astype(BF16)], axis=1)
            filled = jnp.dot(form[...], vectors, preferred_element_type=F32)
            bilinear[at] = filled[:, :tile]
            bilinear[at + 1] = filled[:, tile:]
            flat = jnp.dot(flin[...], jnp.concatenate([vectors, vectors], axis=0), preferred_element_type=F32)
            linear[at] = flat[:, :tile]
            linear[at + 1] = flat[:, tile:]
            return carry

        lax.fori_loop(0, (high - low) // 2, pair, 0, unroll=2)

    def applied(off, c, side, row):
        total = linear[row]
        for k in range(width):
            block = bilinear[row, k * width : (k + 1) * width, :]
            total = total + block * jnp.broadcast_to(uf[off, c, side, pl.ds(k, 1), :], (width, tile))
        return total

    def assemble(off, q):
        states = jnp.concatenate([got[q, c, 1] for c in range(CAP)], axis=1)
        ones = jnp.ones((2 * width, CAP * tile), BF16)
        grown = jnp.dot(flux[...], jnp.concatenate([states, ones], axis=0), preferred_element_type=F32)
        for c in range(CAP):
            mats[off, c] = grown[:, c * tile : (c + 1) * tile]

    def neighboured(off, c, vf):
        row = nbr_row[off * CAP + c]
        total = -speed[off, pl.ds(c, 1), :] * vf[row]
        for j in range(width):
            block = mats[off, c, j * width : (j + 1) * width, :]
            total = total + block * jnp.broadcast_to(vf[row, pl.ds(j, 1), :], (width, tile))
        return total

    def first_block(off, q):
        link(off, q)
        unpack(off, q)
        for c in range(CAP):
            row = jnp.minimum(got_meta[q, c], rows - 1)
            nbr = got_meta[q, CAP + c]
            jump = speed[off, pl.ds(c, 1), :] * (vf1[row] - vf1[nbr])
            chain(off, c, (applied(off, c, 0, row) + jump) + applied(off, c, 1, nbr))

    def source(off):
        near = jnp.minimum(w, owners - 1 - w)
        apart = jnp.where(off <= 2 * near, (off + 1) // 2, off - near)
        below = jnp.where(off <= 2 * near, lax.rem(off, 2) == 1, 2 * w >= owners)
        return jnp.where(below, w - apart, w + apart)

    def chain(off, c, term):
        acc[first_slot + off * CAP + c] = term + acc[before[off * CAP + c]]

    def run(in_sem):
        loads = [
            pltpu.make_async_copy(a, b, in_sem.at[i])
            for i, (a, b) in enumerate(
                (
                    (dest_hbm, dest_ref),
                    (row_hbm, row_ref),
                    (nbr_hbm, nbr_ref),
                    (fo_hbm, fo),
                    (fn_hbm, fn),
                    (halo_hbm, halo_ref),
                    (res_hbm, res),
                    (quad_hbm, quad),
                    (lin_hbm, lin),
                    (state_hbm, state),
                    (tau_hbm, tau),
                    (rate_hbm, rate),
                    (weight_hbm, weight_ref),
                )
            )
        ]
        for load in loads[:5]:
            load.start()
        each(1, owners, greet)

        @pl.when(jnp.logical_not(even))
        def _():
            signal(barrier, s - 1, w)

            @pl.when(has_up)
            def _():
                signal(barrier, s + 1, w)

        for load in loads[5:]:
            load.start()
        around = jnp.where(has_down, 1, 0) + jnp.where(has_up, 1, 0)
        greeted = w + jnp.where(even, around, 0)

        @pl.when(greeted > 0)
        def _():
            pl.semaphore_wait(barrier, greeted)

        each(1, owners, answer)

        @pl.when(even)
        def _():
            @pl.when(has_down)
            def _():
                signal(halo_ready.at[1], s - 1, w)

            @pl.when(has_up)
            def _():
                signal(halo_ready.at[0], s + 1, w)

        for load in loads[:5]:
            load.wait()
        each(1, owners, send_lower)
        loads[5].wait()
        loads[6].wait()

        def round_rows(r, carry):
            vf1[r] = res[r].astype(BF16).astype(F32)
            return carry

        lax.fori_loop(0, rows, round_rows, 0, unroll=4)
        for h in range(halo):
            stage[0, 0, h] = vf1[halo_ref[0, 0, h]].astype(BF16)
            stage[0, 1, h] = vf1[halo_ref[0, 1, h]].astype(BF16)

        @pl.when(even)
        def _():
            send_halo(0)

        each(1, owners, fill_higher)
        fill(w, True)
        send_higher(1)

        for r in range(rows + 1):
            latest[r] = r
        acc[rows] = jnp.zeros((width, tile), F32)
        for vf in (vf1, vf2):

            @pl.when(s == 0)
            def _():
                vf[pl.ds(rows, halo)] = jnp.zeros((halo, width, tile), F32)

            @pl.when(s == slabs - 1)
            def _():
                vf[pl.ds(rows + halo, halo)] = jnp.zeros((halo, width, tile), F32)

        loads[7].wait()
        loads[8].wait()
        at = lax.broadcasted_iota(jnp.int32, (wide, wide), 0)
        column = lax.broadcasted_iota(jnp.int32, (wide, wide), 1)
        swap = jnp.where(column == lax.rem(at, width) * width + at // width, 1.0, 0.0).astype(BF16)
        flux[:, :width] = (
            lax.dot_general(swap, quad[...], (((1,), (1,)), ((), ())), preferred_element_type=F32) * 0.5
        ).astype(BF16)
        half_lin = lin[...] * 0.5
        high = half_lin.astype(BF16)
        low = (half_lin - high.astype(F32)).astype(BF16)
        at = lax.broadcasted_iota(jnp.int32, (wide, width), 0)
        column = lax.broadcasted_iota(jnp.int32, (wide, width), 1)
        pick = jnp.where(column == lax.rem(at, width), 1.0, 0.0).astype(BF16)
        keep = column == at // width
        flin[:, :width] = high
        flin[:, width:] = low
        for i, term in enumerate((high, low)):
            flux[:, (1 + i) * width : (2 + i) * width] = jnp.where(
                keep, jnp.dot(pick, term, preferred_element_type=F32), 0.0
            ).astype(BF16)
        repeat = jnp.where(column == at // width, 1.0, 0.0).astype(BF16)
        each_state = jnp.dot(repeat, quad[...], preferred_element_type=F32) * 0.5
        at = lax.broadcasted_iota(jnp.int32, (wide, wide), 0)
        column = lax.broadcasted_iota(jnp.int32, (wide, wide), 1)
        each_state = jnp.where(column // width == lax.rem(at, width), each_state, 0.0).astype(BF16)
        at = lax.broadcasted_iota(jnp.int32, (wide, width), 0)
        column = lax.broadcasted_iota(jnp.int32, (wide, width), 1)
        gather = jnp.where(column == lax.rem(at, width), 1.0, 0.0).astype(BF16)
        form[...] = jnp.dot(each_state, gather, preferred_element_type=F32).astype(BF16)

        @pl.when(jnp.logical_not(even))
        def _():
            pl.semaphore_wait(halo_ready.at[0], 1)
            down_copy(0).start()

            @pl.when(has_up)
            def _():
                pl.semaphore_wait(halo_ready.at[1], 1)
                up_copy(0).start()

        for load in loads[9:]:
            load.wait()

    pl.run_scoped(run, pltpu.SemaphoreType.DMA((13,)))

    sub = lax.broadcasted_iota(jnp.int32, (width, tile), 0)
    relax = jnp.where(sub == 14, 1.0, 0.0) - jnp.where(sub == 15, 1.0, 0.0)
    mixture = jnp.zeros((width, tile), F32)
    for m in range(nspec):
        mixture = jnp.where(sub == m, weight_ref[m], mixture)

    def prepare(r, carry):
        u = state[r].astype(F32)
        inv = 1.0 / tau[pl.ds(r, 1), :]
        rho = jnp.sum(mixture * u, axis=0, keepdims=True) * inv
        gap = jnp.sum(relax * u, axis=0, keepdims=True) * inv
        coef[r] = gap * mixture + rho * relax
        return carry

    lax.fori_loop(0, rows, prepare, 0, unroll=4)

    def diagonal(vf):
        def one(r, carry):
            v = vf[r]
            change = jnp.sum(coef[r] * v, axis=0, keepdims=True)
            acc[r] = rate[pl.ds(r, 1), :] * v + relax * change
            return carry

        lax.fori_loop(0, rows, one, 0, unroll=4)

    diagonal(vf1)
    contract(0, rows, vf1)
    each(2, owners, send_higher)

    take_halo(0, vf1)
    contract(rows, rows + 2 * halo, vf1)
    first_block(0, w)

    def first_part(off, carry):
        q = source(off)
        pltpu.make_async_copy(got_meta.at[q], got_meta.at[q], meta_recv.at[order(q)]).wait()
        pltpu.make_async_copy(got.at[q], got.at[q], face_recv.at[order(q)]).wait()
        first_block(off, q)
        return carry

    lax.fori_loop(1, owners, first_part, 0)

    for h in range(halo):
        stage[1, 1, h] = acc[latest[halo_ref[0, 1, h]]].astype(BF16)
        stage[1, 0, h] = acc[latest[halo_ref[0, 0, h]]].astype(BF16)
    send_halo(1)
    for r in range(rows):
        value = acc[latest[r]]
        outv1[r] = value
        vf2[r] = value.astype(BF16).astype(F32)
    diagonal(vf2)
    contract(0, rows, vf2)

    def second_own(off, carry):
        for c in range(CAP):
            row = own_row[off * CAP + c]
            part[off * CAP + c] = applied(off, c, 0, row) + speed[off, pl.ds(c, 1), :] * vf2[row]
        assemble(off, source(off))
        return carry

    lax.fori_loop(0, owners, second_own, 0)
    pltpu.make_async_copy(faces.at[pl.ds(0, owners - 1)], faces.at[pl.ds(0, owners - 1)], face_send).wait()
    pltpu.make_async_copy(meta.at[pl.ds(0, owners - 1)], meta.at[pl.ds(0, owners - 1)], meta_send).wait()
    take_halo(1, vf2)

    def second_nbr(off, carry):
        for c in range(CAP):
            chain(off, c, part[off * CAP + c] + neighboured(off, c, vf2))
        return carry

    lax.fori_loop(0, owners, second_nbr, 0, unroll=4)
    for r in range(rows):
        outv2[r] = acc[latest[r]]
    settle(halo_send, stage, stage.at[0])


def store(a, b, c, d, sem):
    first = pltpu.make_async_copy(a, c, sem.at[0])
    second = pltpu.make_async_copy(b, d, sem.at[1])
    first.start()
    second.start()
    first.wait()
    second.wait()


def solution(mesh):
    owners = mesh.shape["wide"]
    slabs = mesh.shape["slab"]

    def on_device(fo, fn, lin, quad, weight, state, tau, rate, res, dest, row, nbr, halo_list):
        count, width, tile = fo.shape
        rows = res.shape[0]
        halo = halo_list.shape[2]
        hbm = pl.BlockSpec(memory_space=pltpu.MemorySpace.HBM)
        vmem = pl.BlockSpec(memory_space=pltpu.MemorySpace.VMEM)
        dma = pltpu.SemaphoreType.DMA
        row_set = (rows, width, tile)
        products = pl.pallas_call(
            functools.partial(kernel, owners, slabs),
            out_shape=(pltpu.VMEM(row_set, F32), pltpu.VMEM(row_set, F32)),
            in_specs=[hbm] * 13,
            out_specs=(vmem, vmem),
            scratch_shapes=[
                pltpu.VMEM(fo.shape, BF16),
                pltpu.VMEM(fn.shape, BF16),
                pltpu.VMEM(lin.shape, F32),
                pltpu.VMEM(quad.shape, BF16),
                pltpu.VMEM(state.shape, BF16),
                pltpu.VMEM(tau.shape, F32),
                pltpu.VMEM(rate.shape, F32),
                pltpu.VMEM(row_set, F32),
                pltpu.VMEM((owners, CAP, 2, width, tile), BF16),
                pltpu.VMEM((owners, CAP, 2, width, tile), BF16),
                pltpu.VMEM((owners, 8, tile), F32),
                pltpu.SMEM((owners, 2 * CAP), jnp.int32),
                pltpu.SMEM((owners, 2 * CAP), jnp.int32),
                pltpu.VMEM((owners, CAP, 2, width, tile), F32),
                pltpu.VMEM((width * width, 3 * width), BF16),
                pltpu.VMEM((width * width, width), BF16),
                pltpu.VMEM((rows + 2 * halo, width * width, tile), F32),
                pltpu.VMEM((rows + 2 * halo, width, tile), F32),
                pltpu.VMEM((width, 2 * width), BF16),
                pltpu.VMEM((owners, CAP, width * width, tile), F32),
                pltpu.VMEM(row_set, F32),
                pltpu.VMEM((rows + 1 + owners * CAP, width, tile), F32),
                pltpu.VMEM((owners * CAP, width, tile), F32),
                pltpu.VMEM((rows + 2 * halo, width, tile), F32),
                pltpu.VMEM((rows + 2 * halo, width, tile), F32),
                pltpu.VMEM((2, 2, halo, width, tile), BF16),
                pltpu.VMEM((2, 2, halo, width, tile), BF16),
                dma(()),
                dma((owners - 1,)),
                dma(()),
                dma((owners - 1,)),
                dma(()),
                dma((2,)),
                pltpu.SemaphoreType.REGULAR((owners - 1,)),
                pltpu.SemaphoreType.REGULAR((2,)),
                pltpu.SMEM(weight.shape, F32),
                pltpu.SMEM((count,), jnp.int32),
                pltpu.SMEM(row.shape, jnp.int32),
                pltpu.SMEM(nbr.shape, jnp.int32),
                pltpu.SMEM(halo_list.shape, jnp.int32),
                pltpu.SMEM((rows + 1,), jnp.int32),
                pltpu.SMEM((owners * CAP,), jnp.int32),
                pltpu.SMEM((owners * CAP,), jnp.int32),
                pltpu.SMEM((owners * CAP,), jnp.int32),
            ],
            compiler_params=pltpu.CompilerParams(collective_id=0, has_side_effects=True),
        )(fo, fn, lin, quad, weight, state, tau, rate, res, dest.reshape(count), row, nbr, halo_list)
        return pl.pallas_call(
            store,
            out_shape=(jax.ShapeDtypeStruct(row_set, F32), jax.ShapeDtypeStruct(row_set, F32)),
            in_specs=[vmem, vmem],
            out_specs=(hbm, hbm),
            scratch_shapes=[dma((2,))],
        )(*[pltpu.with_memory_space_constraint(x, pltpu.MemorySpace.VMEM) for x in products])

    every = ("slab", "wide")
    cube, flat = P(every, None, None), P(every, None)
    return jax.shard_map(
        on_device,
        mesh=mesh,
        in_specs=(cube, cube, P(), P(), P(), cube, flat, flat, cube, flat, P(every), P(every), cube),
        out_specs=(cube, cube),
        check_vma=False,
    )
```

```python
import functools

import jax
import jax.numpy as jnp
from jax import lax
from jax.experimental import pallas as pl
from jax.experimental.pallas import tpu as pltpu
from jax.sharding import PartitionSpec as P

CAP = 4
MESH = pl.DeviceIdType.MESH
F32 = jnp.float32
BF16 = jnp.bfloat16


def each(low, high, body):
    if high - low <= 8:
        for i in range(low, high):
            body(i)
    else:

        def step(i, carry):
            body(i)
            return carry

        lax.fori_loop(low, high, step, 0)


def kernel(
    owners,
    slabs,
    fo_hbm,
    fn_hbm,
    lin_hbm,
    quad_hbm,
    weight_hbm,
    state_hbm,
    tau_hbm,
    rate_hbm,
    res_hbm,
    dest_hbm,
    row_hbm,
    nbr_hbm,
    halo_hbm,
    outv1,
    outv2,
    fo,
    fn,
    lin,
    quad,
    state,
    tau,
    rate,
    res,
    faces,
    got,
    speed,
    meta,
    got_meta,
    uf,
    flux,
    form,
    bilinear,
    linear,
    flin,
    mats,
    coef,
    acc,
    part,
    vf1,
    vf2,
    stage,
    land,
    face_recv,
    meta_recv,
    halo_recv,
    ready,
    halo_ready,
    weight_ref,
    dest_ref,
    row_ref,
    nbr_ref,
    halo_ref,
    latest,
    before,
    own_row,
    nbr_row,
    picked,
):
    def scope(in_sem, face_send, meta_send, halo_send):
        s = lax.axis_index("slab")
        w = lax.axis_index("wide")
        count, width, tile = fo.shape
        rows = res.shape[0]
        nspec = weight_ref.shape[0]
        halo = halo_ref.shape[2]
        wide = width * width
        first_slot = rows + 1

        barrier = pltpu.get_barrier_semaphore()
        even = lax.rem(s, 2) == 0
        has_down = s > 0
        has_up = s < slabs - 1
        inner = has_down & has_up

        def signal(sem, slab, wide):
            pl.semaphore_signal(sem, inc=1, device_id=(slab, wide), device_id_type=MESH)

        def greet(off):
            @pl.when(w + off < owners)
            def _():
                signal(barrier, s, w + off)

        def answer(off):
            @pl.when(w - off >= 0)
            def _():
                signal(ready.at[w - 1], s, w - off)

        bits = count.bit_length()
        mask = (1 << bits) - 1

        def picks(peer):
            packed = jnp.int32(0)
            for t in range(count):
                packed = jnp.where(dest_ref[t] == peer, packed * (1 << bits) + (t + 1), packed)
            return [(packed >> (bits * c)) & mask for c in range(CAP)]

        def fill_meta(d, place):
            found = picks(d)
            for c in range(CAP):
                source = jnp.maximum(found[c] - 1, 0)
                picked[d, c] = source
                place[d, c] = jnp.where(found[c] > 0, row_ref[source], rows)
                place[d, CAP + c] = jnp.where(found[c] > 0, nbr_ref[source], 0)

        def fill_faces(d, place):
            for c in range(CAP):
                source = picked[d, c]
                place[d, c, 0] = fo[source]
                place[d, c, 1] = fn[source]

        def order(peer):
            return peer - jnp.where(peer > w, 1, 0)

        def face_copy(peer):
            return pltpu.make_async_remote_copy(
                src_ref=faces.at[peer],
                dst_ref=got.at[w],
                send_sem=face_send,
                recv_sem=face_recv.at[w - jnp.where(w > peer, 1, 0)],
                device_id=(s, peer),
                device_id_type=MESH,
            )

        def meta_copy(peer):
            return pltpu.make_async_remote_copy(
                src_ref=meta.at[peer],
                dst_ref=got_meta.at[w],
                send_sem=meta_send,
                recv_sem=meta_recv.at[w - jnp.where(w > peer, 1, 0)],
                device_id=(s, peer),
                device_id_type=MESH,
            )

        def name_lower(peer):
            @pl.when(peer < w)
            def _():
                fill_meta(peer, meta)
                meta_copy(peer).start()

        def send_lower(peer):
            @pl.when(peer < w)
            def _():
                fill_faces(peer, faces)
                face_copy(peer).start()

        def fill_higher(off):
            @pl.when(w + off < owners)
            def _():
                fill_meta(w + off, meta)
                fill_faces(w + off, faces)

        def send_higher(off):
            peer = w + off

            @pl.when(peer < owners)
            def _():
                pl.semaphore_wait(ready.at[peer - 1], 1)
                meta_copy(peer).start()
                face_copy(peer).start()

        def up_copy(phase):
            return pltpu.make_async_remote_copy(
                src_ref=stage.at[phase, 0],
                dst_ref=land.at[phase, 0],
                send_sem=halo_send,
                recv_sem=halo_recv.at[phase],
                device_id=(s + 1, w),
                device_id_type=MESH,
            )

        def down_copy(phase):
            return pltpu.make_async_remote_copy(
                src_ref=stage.at[phase, 1],
                dst_ref=land.at[phase, 1],
                send_sem=halo_send,
                recv_sem=halo_recv.at[phase],
                device_id=(s - 1, w),
                device_id_type=MESH,
            )

        def send_halo(phase):
            @pl.when(has_down)
            def _():
                down_copy(phase).start()

            @pl.when(has_up)
            def _():
                up_copy(phase).start()

        def settle(sem, many, few):
            @pl.when(inner)
            def _():
                pltpu.make_async_copy(many, many, sem).wait()

            @pl.when(jnp.logical_not(inner))
            def _():
                pltpu.make_async_copy(few, few, sem).wait()

        def take_halo(phase, vf):
            settle(halo_recv.at[phase], land.at[phase], land.at[phase, 0])

            @pl.when(has_down)
            def _():
                for h in range(halo):
                    vf[rows + h] = land[phase, 0, h].astype(F32)

            @pl.when(has_up)
            def _():
                for h in range(halo):
                    vf[rows + halo + h] = land[phase, 1, h].astype(F32)

        def link(off, q):
            named = [got_meta[q, c] for c in range(CAP)]
            at = first_slot + off * CAP
            for c in range(CAP):
                last = latest[named[c]]
                for e in range(c):
                    last = jnp.where(named[e] == named[c], at + e, last)
                before[off * CAP + c] = last
                own_row[off * CAP + c] = jnp.minimum(named[c], rows - 1)
                nbr_row[off * CAP + c] = got_meta[q, CAP + c]
            for r in range(rows):
                last = latest[r]
                for c in range(CAP):
                    last = jnp.where(named[c] == r, at + c, last)
                latest[r] = last

        def unpack(off, q):
            for c in range(CAP):
                own = got[q, c, 0].astype(F32)
                nbr = got[q, c, 1].astype(F32)
                uf[off, c, 0] = own
                uf[off, c, 1] = nbr
                square = jnp.sum(own * own + nbr * nbr, axis=0, keepdims=True)
                speed[off, pl.ds(c, 1), :] = 0.5 + 0.5 * jnp.sqrt(square * (0.5 / width))

        def contract(low, high, vf):
            def some(i, carry):
                at = low + 4 * i
                vectors = jnp.concatenate([vf[at + n].astype(BF16) for n in range(4)], axis=1)
                filled = jnp.dot(form[...], vectors, preferred_element_type=F32)
                flat = jnp.dot(flin[...], jnp.concatenate([vectors, vectors], axis=0), preferred_element_type=F32)
                for n in range(4):
                    bilinear[at + n] = filled[:, n * tile : (n + 1) * tile]
                    linear[at + n] = flat[:, n * tile : (n + 1) * tile]
                return carry

            lax.fori_loop(0, (high - low) // 4, some, 0)

        def applied(off, c, side, row):
            total = linear[row]
            for k in range(width):
                block = bilinear[row, k * width : (k + 1) * width, :]
                total = total + block * jnp.broadcast_to(uf[off, c, side, pl.ds(k, 1), :], (width, tile))
            return total

        def assemble(off, q):
            states = jnp.concatenate([got[q, c, 1] for c in range(CAP)], axis=1)
            ones = jnp.ones((2 * width, CAP * tile), BF16)
            grown = jnp.dot(flux[...], jnp.concatenate([states, ones], axis=0), preferred_element_type=F32)
            for c in range(CAP):
                mats[off, c] = grown[:, c * tile : (c + 1) * tile]

        def neighboured(off, c, vf):
            row = nbr_row[off * CAP + c]
            total = -speed[off, pl.ds(c, 1), :] * vf[row]
            for j in range(width):
                block = mats[off, c, j * width : (j + 1) * width, :]
                total = total + block * jnp.broadcast_to(vf[row, pl.ds(j, 1), :], (width, tile))
            return total

        def first_block(off, q):
            link(off, q)
            unpack(off, q)
            for c in range(CAP):
                row = jnp.minimum(got_meta[q, c], rows - 1)
                nbr = got_meta[q, CAP + c]
                jump = speed[off, pl.ds(c, 1), :] * (vf1[row] - vf1[nbr])
                chain(off, c, (applied(off, c, 0, row) + jump) + applied(off, c, 1, nbr))

        def source(off):
            near = jnp.minimum(w, owners - 1 - w)
            apart = jnp.where(off <= 2 * near, (off + 1) // 2, off - near)
            below = jnp.where(off <= 2 * near, lax.rem(off, 2) == 1, 2 * w >= owners)
            return jnp.where(below, w - apart, w + apart)

        def chain(off, c, term):
            acc[first_slot + off * CAP + c] = term + acc[before[off * CAP + c]]

        def run():
            loads = [
                pltpu.make_async_copy(a, b, in_sem.at[i])
                for i, (a, b) in enumerate(
                    (
                        (dest_hbm, dest_ref),
                        (row_hbm, row_ref),
                        (nbr_hbm, nbr_ref),
                        (fo_hbm, fo),
                        (fn_hbm, fn),
                        (halo_hbm, halo_ref),
                        (res_hbm, res),
                        (quad_hbm, quad),
                        (lin_hbm, lin),
                        (state_hbm, state),
                        (tau_hbm, tau),
                        (rate_hbm, rate),
                        (weight_hbm, weight_ref),
                    )
                )
            ]
            for load in loads[:5]:
                load.start()
            each(1, owners, greet)

            @pl.when(jnp.logical_not(even))
            def _():
                signal(barrier, s - 1, w)

                @pl.when(has_up)
                def _():
                    signal(barrier, s + 1, w)

            for load in loads[5:]:
                load.start()
            around = jnp.where(has_down, 1, 0) + jnp.where(has_up, 1, 0)
            greeted = w + jnp.where(even, around, 0)

            @pl.when(greeted > 0)
            def _():
                pl.semaphore_wait(barrier, greeted)

            each(1, owners, answer)

            @pl.when(even)
            def _():
                @pl.when(has_down)
                def _():
                    signal(halo_ready, s - 1, w)

                @pl.when(has_up)
                def _():
                    signal(halo_ready, s + 1, w)

            for load in loads[:3]:
                load.wait()
            each(0, owners - 1, name_lower)
            for load in loads[3:5]:
                load.wait()
            each(0, owners - 1, send_lower)

            loads[5].wait()
            loads[6].wait()

            def round_rows(r, carry):
                vf1[r] = res[r].astype(BF16).astype(F32)
                return carry

            lax.fori_loop(0, rows, round_rows, 0, unroll=4)
            for h in range(halo):
                stage[0, 0, h] = vf1[halo_ref[0, 0, h]].astype(BF16)
                stage[0, 1, h] = vf1[halo_ref[0, 1, h]].astype(BF16)

            @pl.when(even)
            def _():
                send_halo(0)

            each(1, owners, fill_higher)
            fill_meta(w, got_meta)
            fill_faces(w, got)
            send_higher(1)

            for r in range(rows + 1):
                latest[r] = r
            acc[rows] = jnp.zeros((width, tile), F32)
            for vf in (vf1, vf2):

                @pl.when(s == 0)
                def _():
                    vf[pl.ds(rows, halo)] = jnp.zeros((halo, width, tile), F32)

                @pl.when(s == slabs - 1)
                def _():
                    vf[pl.ds(rows + halo, halo)] = jnp.zeros((halo, width, tile), F32)

            loads[7].wait()
            loads[8].wait()
            at = lax.broadcasted_iota(jnp.int32, (wide, wide), 0)
            column = lax.broadcasted_iota(jnp.int32, (wide, wide), 1)
            swap = jnp.where(column == lax.rem(at, width) * width + at // width, 1.0, 0.0).astype(BF16)
            flux[:, :width] = (
                lax.dot_general(swap, quad[...], (((1,), (1,)), ((), ())), preferred_element_type=F32) * 0.5
            ).astype(BF16)
            half_lin = lin[...] * 0.5
            high = half_lin.astype(BF16)
            low = (half_lin - high.astype(F32)).astype(BF16)
            at = lax.broadcasted_iota(jnp.int32, (wide, width), 0)
            column = lax.broadcasted_iota(jnp.int32, (wide, width), 1)
            pick = jnp.where(column == lax.rem(at, width), 1.0, 0.0).astype(BF16)
            keep = column == at // width
            flin[:, :width] = high
            flin[:, width:] = low
            for i, term in enumerate((high, low)):
                flux[:, (1 + i) * width : (2 + i) * width] = jnp.where(
                    keep, jnp.dot(pick, term, preferred_element_type=F32), 0.0
                ).astype(BF16)
            repeat = jnp.where(column == at // width, 1.0, 0.0).astype(BF16)
            each_state = jnp.dot(repeat, quad[...], preferred_element_type=F32) * 0.5
            at = lax.broadcasted_iota(jnp.int32, (wide, wide), 0)
            column = lax.broadcasted_iota(jnp.int32, (wide, wide), 1)
            each_state = jnp.where(column // width == lax.rem(at, width), each_state, 0.0).astype(BF16)
            at = lax.broadcasted_iota(jnp.int32, (wide, width), 0)
            column = lax.broadcasted_iota(jnp.int32, (wide, width), 1)
            gather = jnp.where(column == lax.rem(at, width), 1.0, 0.0).astype(BF16)
            form[...] = jnp.dot(each_state, gather, preferred_element_type=F32).astype(BF16)

            @pl.when(jnp.logical_not(even))
            def _():
                pl.semaphore_wait(halo_ready, around)
                send_halo(0)

            for load in loads[9:]:
                load.wait()

        run()

        sub = lax.broadcasted_iota(jnp.int32, (width, tile), 0)
        relax = jnp.where(sub == 14, 1.0, 0.0) - jnp.where(sub == 15, 1.0, 0.0)
        mixture = jnp.zeros((width, tile), F32)
        for m in range(nspec):
            mixture = jnp.where(sub == m, weight_ref[m], mixture)

        def prepare(r, carry):
            u = state[r].astype(F32)
            inv = 1.0 / tau[pl.ds(r, 1), :]
            rho = jnp.sum(mixture * u, axis=0, keepdims=True) * inv
            gap = jnp.sum(relax * u, axis=0, keepdims=True) * inv
            coef[r] = gap * mixture + rho * relax
            return carry

        lax.fori_loop(0, rows, prepare, 0, unroll=4)

        def diagonal(vf):
            def one(r, carry):
                v = vf[r]
                change = jnp.sum(coef[r] * v, axis=0, keepdims=True)
                acc[r] = rate[pl.ds(r, 1), :] * v + relax * change
                return carry

            lax.fori_loop(0, rows, one, 0, unroll=4)

        diagonal(vf1)
        each(2, owners, send_higher)

        contract(0, rows, vf1)
        take_halo(0, vf1)
        contract(rows, rows + 2 * halo, vf1)
        first_block(0, w)

        def first_part(off, carry):
            q = source(off)
            pltpu.make_async_copy(got_meta.at[q], got_meta.at[q], meta_recv.at[order(q)]).wait()
            pltpu.make_async_copy(got.at[q], got.at[q], face_recv.at[order(q)]).wait()
            first_block(off, q)
            return carry

        lax.fori_loop(1, owners, first_part, 0)

        for h in range(halo):
            stage[1, 1, h] = acc[latest[halo_ref[0, 1, h]]].astype(BF16)
            stage[1, 0, h] = acc[latest[halo_ref[0, 0, h]]].astype(BF16)
        send_halo(1)
        for r in range(rows):
            value = acc[latest[r]]
            outv1[r] = value
            vf2[r] = value.astype(BF16).astype(F32)
        diagonal(vf2)
        contract(0, rows, vf2)

        def second_own(off, carry):
            for c in range(CAP):
                row = own_row[off * CAP + c]
                part[off * CAP + c] = applied(off, c, 0, row) + speed[off, pl.ds(c, 1), :] * vf2[row]
            assemble(off, source(off))
            return carry

        lax.fori_loop(0, owners, second_own, 0)
        pltpu.make_async_copy(faces.at[pl.ds(0, owners - 1)], faces.at[pl.ds(0, owners - 1)], face_send).wait()
        pltpu.make_async_copy(meta.at[pl.ds(0, owners - 1)], meta.at[pl.ds(0, owners - 1)], meta_send).wait()
        take_halo(1, vf2)

        def second_nbr(off, carry):
            for c in range(CAP):
                chain(off, c, part[off * CAP + c] + neighboured(off, c, vf2))
            return carry

        lax.fori_loop(0, owners, second_nbr, 0, unroll=4)
        for r in range(rows):
            outv2[r] = acc[latest[r]]
        settle(halo_send, stage, stage.at[0])

    dma = pltpu.SemaphoreType.DMA
    pl.run_scoped(scope, dma((13,)), dma(()), dma(()), dma(()))


def store(a, b, c, d, sem):
    first = pltpu.make_async_copy(a, c, sem.at[0])
    second = pltpu.make_async_copy(b, d, sem.at[1])
    first.start()
    second.start()
    first.wait()
    second.wait()


def solution(mesh):
    owners = mesh.shape["wide"]
    slabs = mesh.shape["slab"]

    def on_device(fo, fn, lin, quad, weight, state, tau, rate, res, dest, row, nbr, halo_list):
        count, width, tile = fo.shape
        rows = res.shape[0]
        halo = halo_list.shape[2]
        hbm = pl.BlockSpec(memory_space=pltpu.MemorySpace.HBM)
        vmem = pl.BlockSpec(memory_space=pltpu.MemorySpace.VMEM)
        dma = pltpu.SemaphoreType.DMA
        row_set = (rows, width, tile)
        products = pl.pallas_call(
            functools.partial(kernel, owners, slabs),
            out_shape=(pltpu.VMEM(row_set, F32), pltpu.VMEM(row_set, F32)),
            in_specs=[hbm] * 13,
            out_specs=(vmem, vmem),
            scratch_shapes=[
                pltpu.VMEM(fo.shape, BF16),
                pltpu.VMEM(fn.shape, BF16),
                pltpu.VMEM(lin.shape, F32),
                pltpu.VMEM(quad.shape, BF16),
                pltpu.VMEM(state.shape, BF16),
                pltpu.VMEM(tau.shape, F32),
                pltpu.VMEM(rate.shape, F32),
                pltpu.VMEM(row_set, F32),
                pltpu.VMEM((owners, CAP, 2, width, tile), BF16),
                pltpu.VMEM((owners, CAP, 2, width, tile), BF16),
                pltpu.VMEM((owners, 8, tile), F32),
                pltpu.SMEM((owners, 2 * CAP), jnp.int32),
                pltpu.SMEM((owners, 2 * CAP), jnp.int32),
                pltpu.VMEM((owners, CAP, 2, width, tile), F32),
                pltpu.VMEM((width * width, 3 * width), BF16),
                pltpu.VMEM((width * width, width), BF16),
                pltpu.VMEM((rows + 2 * halo, width * width, tile), F32),
                pltpu.VMEM((rows + 2 * halo, width, tile), F32),
                pltpu.VMEM((width, 2 * width), BF16),
                pltpu.VMEM((owners, CAP, width * width, tile), F32),
                pltpu.VMEM(row_set, F32),
                pltpu.VMEM((rows + 1 + owners * CAP, width, tile), F32),
                pltpu.VMEM((owners * CAP, width, tile), F32),
                pltpu.VMEM((rows + 2 * halo, width, tile), F32),
                pltpu.VMEM((rows + 2 * halo, width, tile), F32),
                pltpu.VMEM((2, 2, halo, width, tile), BF16),
                pltpu.VMEM((2, 2, halo, width, tile), BF16),
                dma((owners - 1,)),
                dma((owners - 1,)),
                dma((2,)),
                pltpu.SemaphoreType.REGULAR((owners - 1,)),
                pltpu.SemaphoreType.REGULAR,
                pltpu.SMEM(weight.shape, F32),
                pltpu.SMEM((count,), jnp.int32),
                pltpu.SMEM(row.shape, jnp.int32),
                pltpu.SMEM(nbr.shape, jnp.int32),
                pltpu.SMEM(halo_list.shape, jnp.int32),
                pltpu.SMEM((rows + 1,), jnp.int32),
                pltpu.SMEM((owners * CAP,), jnp.int32),
                pltpu.SMEM((owners * CAP,), jnp.int32),
                pltpu.SMEM((owners * CAP,), jnp.int32),
                pltpu.SMEM((owners, CAP), jnp.int32),
            ],
            compiler_params=pltpu.CompilerParams(collective_id=0, has_side_effects=True),
        )(fo, fn, lin, quad, weight, state, tau, rate, res, dest.reshape(count), row, nbr, halo_list)
        return pl.pallas_call(
            store,
            out_shape=(jax.ShapeDtypeStruct(row_set, F32), jax.ShapeDtypeStruct(row_set, F32)),
            in_specs=[vmem, vmem],
            out_specs=(hbm, hbm),
            scratch_shapes=[dma((2,))],
        )(*[pltpu.with_memory_space_constraint(x, pltpu.MemorySpace.VMEM) for x in products])

    every = ("slab", "wide")
    cube, flat = P(every, None, None), P(every, None)
    return jax.shard_map(
        on_device,
        mesh=mesh,
        in_specs=(cube, cube, P(), P(), P(), cube, flat, flat, cube, flat, P(every), P(every), cube),
        out_specs=(cube, cube),
        check_vma=False,
    )
```

```python
import functools

import jax
import jax.numpy as jnp
from jax import lax
from jax.experimental import pallas as pl
from jax.experimental.pallas import tpu as pltpu
from jax.sharding import PartitionSpec as P

CAP = 4
MESH = pl.DeviceIdType.MESH
F32 = jnp.float32
BF16 = jnp.bfloat16


def each(low, high, body):
    if high - low <= 8:
        for i in range(low, high):
            body(i)
    else:

        def step(i, carry):
            body(i)
            return carry

        lax.fori_loop(low, high, step, 0)


def kernel(
    owners,
    slabs,
    fo_hbm,
    fn_hbm,
    lin_hbm,
    quad_hbm,
    weight_hbm,
    state_hbm,
    tau_hbm,
    rate_hbm,
    res_hbm,
    dest_hbm,
    row_hbm,
    nbr_hbm,
    halo_hbm,
    outv1,
    outv2,
    fo,
    fn,
    lin,
    quad,
    state,
    tau,
    rate,
    res,
    faces,
    got,
    speed,
    meta,
    got_meta,
    uf,
    flux,
    form,
    bilinear,
    linear,
    flin,
    mats,
    coef,
    acc,
    part,
    vf1,
    vf2,
    stage,
    land,
    face_recv,
    meta_recv,
    halo_recv,
    ready,
    halo_ready,
    weight_ref,
    dest_ref,
    row_ref,
    nbr_ref,
    halo_ref,
    latest,
    before,
    own_row,
    nbr_row,
    picked,
):
    def scope(in_sem, face_send, meta_send, halo_send):
        s = lax.axis_index("slab")
        w = lax.axis_index("wide")
        count, width, tile = fo.shape
        rows = res.shape[0]
        nspec = weight_ref.shape[0]
        halo = halo_ref.shape[2]
        wide = width * width
        first_slot = rows + 1

        barrier = pltpu.get_barrier_semaphore()
        even = lax.rem(s, 2) == 0
        has_down = s > 0
        has_up = s < slabs - 1
        inner = has_down & has_up

        def signal(sem, slab, wide):
            pl.semaphore_signal(sem, inc=1, device_id=(slab, wide), device_id_type=MESH)

        def greet(off):
            @pl.when(w + off < owners)
            def _():
                signal(barrier, s, w + off)

        def answer(off):
            @pl.when(w - off >= 0)
            def _():
                signal(ready.at[w - 1], s, w - off)

        bits = count.bit_length()
        mask = (1 << bits) - 1

        def picks(peer):
            packed = jnp.int32(0)
            for t in range(count):
                packed = jnp.where(dest_ref[t] == peer, packed * (1 << bits) + (t + 1), packed)
            return [(packed >> (bits * c)) & mask for c in range(CAP)]

        def fill_meta(d, place):
            found = picks(d)
            for c in range(CAP):
                source = jnp.maximum(found[c] - 1, 0)
                picked[d, c] = source
                place[d, c] = jnp.where(found[c] > 0, row_ref[source], rows)
                place[d, CAP + c] = jnp.where(found[c] > 0, nbr_ref[source], 0)

        def fill_faces(d, place):
            for c in range(CAP):
                source = picked[d, c]
                place[d, c, 0] = fo[source]
                place[d, c, 1] = fn[source]

        def order(peer):
            return peer - jnp.where(peer > w, 1, 0)

        def face_copy(peer):
            return pltpu.make_async_remote_copy(
                src_ref=faces.at[peer],
                dst_ref=got.at[w],
                send_sem=face_send,
                recv_sem=face_recv.at[w - jnp.where(w > peer, 1, 0)],
                device_id=(s, peer),
                device_id_type=MESH,
            )

        def meta_copy(peer):
            return pltpu.make_async_remote_copy(
                src_ref=meta.at[peer],
                dst_ref=got_meta.at[w],
                send_sem=meta_send,
                recv_sem=meta_recv.at[w - jnp.where(w > peer, 1, 0)],
                device_id=(s, peer),
                device_id_type=MESH,
            )

        def name_lower(peer):
            @pl.when(peer < w)
            def _():
                fill_meta(peer, meta)
                meta_copy(peer).start()

        def send_lower(peer):
            @pl.when(peer < w)
            def _():
                fill_faces(peer, faces)
                face_copy(peer).start()

        def fill_higher(off):
            @pl.when(w + off < owners)
            def _():
                fill_meta(w + off, meta)
                fill_faces(w + off, faces)

        def send_higher(off):
            peer = w + off

            @pl.when(peer < owners)
            def _():
                pl.semaphore_wait(ready.at[peer - 1], 1)
                meta_copy(peer).start()
                face_copy(peer).start()

        def up_copy(phase):
            return pltpu.make_async_remote_copy(
                src_ref=stage.at[phase, 0],
                dst_ref=land.at[phase, 0],
                send_sem=halo_send,
                recv_sem=halo_recv.at[phase],
                device_id=(s + 1, w),
                device_id_type=MESH,
            )

        def down_copy(phase):
            return pltpu.make_async_remote_copy(
                src_ref=stage.at[phase, 1],
                dst_ref=land.at[phase, 1],
                send_sem=halo_send,
                recv_sem=halo_recv.at[phase],
                device_id=(s - 1, w),
                device_id_type=MESH,
            )

        def send_halo(phase):
            @pl.when(has_down)
            def _():
                down_copy(phase).start()

            @pl.when(has_up)
            def _():
                up_copy(phase).start()

        def settle(sem, many, few):
            @pl.when(inner)
            def _():
                pltpu.make_async_copy(many, many, sem).wait()

            @pl.when(jnp.logical_not(inner))
            def _():
                pltpu.make_async_copy(few, few, sem).wait()

        def take_halo(phase, vf):
            settle(halo_recv.at[phase], land.at[phase], land.at[phase, 0])

            @pl.when(has_down)
            def _():
                for h in range(halo):
                    vf[rows + h] = land[phase, 0, h].astype(F32)

            @pl.when(has_up)
            def _():
                for h in range(halo):
                    vf[rows + halo + h] = land[phase, 1, h].astype(F32)

        def link(off, q):
            named = [got_meta[q, c] for c in range(CAP)]
            at = first_slot + off * CAP
            for c in range(CAP):
                last = latest[named[c]]
                for e in range(c):
                    last = jnp.where(named[e] == named[c], at + e, last)
                before[off * CAP + c] = last
                own_row[off * CAP + c] = jnp.minimum(named[c], rows - 1)
                nbr_row[off * CAP + c] = got_meta[q, CAP + c]
            for r in range(rows):
                last = latest[r]
                for c in range(CAP):
                    last = jnp.where(named[c] == r, at + c, last)
                latest[r] = last

        def unpack(off, q):
            for c in range(CAP):
                own = got[q, c, 0].astype(F32)
                nbr = got[q, c, 1].astype(F32)
                uf[off, c, 0] = own
                uf[off, c, 1] = nbr
                square = jnp.sum(own * own + nbr * nbr, axis=0, keepdims=True)
                speed[off, pl.ds(c, 1), :] = 0.5 + 0.5 * jnp.sqrt(square * (0.5 / width))

        def contract(low, high, vf):
            def some(i, carry):
                at = low + 4 * i
                vectors = jnp.concatenate([vf[at + n].astype(BF16) for n in range(4)], axis=1)
                filled = jnp.dot(form[...], vectors, preferred_element_type=F32)
                flat = jnp.dot(flin[...], jnp.concatenate([vectors, vectors], axis=0), preferred_element_type=F32)
                for n in range(4):
                    bilinear[at + n] = filled[:, n * tile : (n + 1) * tile]
                    linear[at + n] = flat[:, n * tile : (n + 1) * tile]
                return carry

            lax.fori_loop(0, (high - low) // 4, some, 0)

        def folded(term, low, high):
            sums = [term(low + n) for n in range(4)]
            for n in range(low + 4, high):
                sums[n % 4] = sums[n % 4] + term(n)
            return (sums[0] + sums[1]) + (sums[2] + sums[3])

        def applied(off, c, side, row):
            def term(k):
                block = bilinear[row, k * width : (k + 1) * width, :]
                return block * jnp.broadcast_to(uf[off, c, side, pl.ds(k, 1), :], (width, tile))

            return linear[row] + folded(term, 0, width)

        def assemble(off, q):
            states = jnp.concatenate([got[q, c, 1] for c in range(CAP)], axis=1)
            ones = jnp.ones((2 * width, CAP * tile), BF16)
            grown = jnp.dot(flux[...], jnp.concatenate([states, ones], axis=0), preferred_element_type=F32)
            for c in range(CAP):
                mats[off, c] = grown[:, c * tile : (c + 1) * tile]

        def neighboured(off, c, vf):
            row = nbr_row[off * CAP + c]

            def term(j):
                block = mats[off, c, j * width : (j + 1) * width, :]
                return block * jnp.broadcast_to(vf[row, pl.ds(j, 1), :], (width, tile))

            return folded(term, 0, width) - speed[off, pl.ds(c, 1), :] * vf[row]

        def first_block(off, q):
            unpack(off, q)
            for c in range(CAP):
                row = jnp.minimum(got_meta[q, c], rows - 1)
                nbr = got_meta[q, CAP + c]
                jump = speed[off, pl.ds(c, 1), :] * (vf1[row] - vf1[nbr])
                chain(off, c, (applied(off, c, 0, row) + jump) + applied(off, c, 1, nbr))

        def source(off):
            near = jnp.minimum(w, owners - 1 - w)
            apart = jnp.where(off <= 2 * near, (off + 1) // 2, off - near)
            below = jnp.where(off <= 2 * near, lax.rem(off, 2) == 1, 2 * w >= owners)
            return jnp.where(below, w - apart, w + apart)

        def chain(off, c, term):
            acc[first_slot + off * CAP + c] = term + acc[before[off * CAP + c]]

        def run():
            loads = [
                pltpu.make_async_copy(a, b, in_sem.at[i])
                for i, (a, b) in enumerate(
                    (
                        (dest_hbm, dest_ref),
                        (row_hbm, row_ref),
                        (nbr_hbm, nbr_ref),
                        (fo_hbm, fo),
                        (fn_hbm, fn),
                        (halo_hbm, halo_ref),
                        (res_hbm, res),
                        (quad_hbm, quad),
                        (lin_hbm, lin),
                        (state_hbm, state),
                        (tau_hbm, tau),
                        (rate_hbm, rate),
                        (weight_hbm, weight_ref),
                    )
                )
            ]
            for load in loads[:5]:
                load.start()
            each(1, owners, greet)

            @pl.when(jnp.logical_not(even))
            def _():
                signal(barrier, s - 1, w)

                @pl.when(has_up)
                def _():
                    signal(barrier, s + 1, w)

            for load in loads[5:]:
                load.start()
            around = jnp.where(has_down, 1, 0) + jnp.where(has_up, 1, 0)
            greeted = w + jnp.where(even, around, 0)

            @pl.when(greeted > 0)
            def _():
                pl.semaphore_wait(barrier, greeted)

            each(1, owners, answer)

            @pl.when(even)
            def _():
                @pl.when(has_down)
                def _():
                    signal(halo_ready, s - 1, w)

                @pl.when(has_up)
                def _():
                    signal(halo_ready, s + 1, w)

            for load in loads[:3]:
                load.wait()
            name_lower(0)
            for load in loads[3:5]:
                load.wait()
            send_lower(0)

            def next_lower(peer):
                name_lower(peer)
                send_lower(peer)

            each(1, owners - 1, next_lower)

            loads[5].wait()
            loads[6].wait()

            def round_rows(r, carry):
                vf1[r] = res[r].astype(BF16).astype(F32)
                return carry

            lax.fori_loop(0, rows, round_rows, 0, unroll=4)
            for h in range(halo):
                stage[0, 0, h] = vf1[halo_ref[0, 0, h]].astype(BF16)
                stage[0, 1, h] = vf1[halo_ref[0, 1, h]].astype(BF16)

            @pl.when(even)
            def _():
                send_halo(0)

            each(1, owners, fill_higher)
            fill_meta(w, got_meta)
            fill_faces(w, got)
            send_higher(1)

            for r in range(rows + 1):
                latest[r] = r
            acc[rows] = jnp.zeros((width, tile), F32)
            for vf in (vf1, vf2):

                @pl.when(s == 0)
                def _():
                    vf[pl.ds(rows, halo)] = jnp.zeros((halo, width, tile), F32)

                @pl.when(s == slabs - 1)
                def _():
                    vf[pl.ds(rows + halo, halo)] = jnp.zeros((halo, width, tile), F32)

            loads[7].wait()
            loads[8].wait()
            at = lax.broadcasted_iota(jnp.int32, (wide, wide), 0)
            column = lax.broadcasted_iota(jnp.int32, (wide, wide), 1)
            swap = jnp.where(column == lax.rem(at, width) * width + at // width, 1.0, 0.0).astype(BF16)
            flux[:, :width] = (
                lax.dot_general(swap, quad[...], (((1,), (1,)), ((), ())), preferred_element_type=F32) * 0.5
            ).astype(BF16)
            half_lin = lin[...] * 0.5
            high = half_lin.astype(BF16)
            low = (half_lin - high.astype(F32)).astype(BF16)
            at = lax.broadcasted_iota(jnp.int32, (wide, width), 0)
            column = lax.broadcasted_iota(jnp.int32, (wide, width), 1)
            pick = jnp.where(column == lax.rem(at, width), 1.0, 0.0).astype(BF16)
            keep = column == at // width
            flin[:, :width] = high
            flin[:, width:] = low
            for i, term in enumerate((high, low)):
                flux[:, (1 + i) * width : (2 + i) * width] = jnp.where(
                    keep, jnp.dot(pick, term, preferred_element_type=F32), 0.0
                ).astype(BF16)
            repeat = jnp.where(column == at // width, 1.0, 0.0).astype(BF16)
            each_state = jnp.dot(repeat, quad[...], preferred_element_type=F32) * 0.5
            at = lax.broadcasted_iota(jnp.int32, (wide, wide), 0)
            column = lax.broadcasted_iota(jnp.int32, (wide, wide), 1)
            each_state = jnp.where(column // width == lax.rem(at, width), each_state, 0.0).astype(BF16)
            at = lax.broadcasted_iota(jnp.int32, (wide, width), 0)
            column = lax.broadcasted_iota(jnp.int32, (wide, width), 1)
            gather = jnp.where(column == lax.rem(at, width), 1.0, 0.0).astype(BF16)
            form[...] = jnp.dot(each_state, gather, preferred_element_type=F32).astype(BF16)

            @pl.when(jnp.logical_not(even))
            def _():
                pl.semaphore_wait(halo_ready, around)
                send_halo(0)

            for load in loads[9:]:
                load.wait()

        run()

        sub = lax.broadcasted_iota(jnp.int32, (width, tile), 0)
        relax = jnp.where(sub == 14, 1.0, 0.0) - jnp.where(sub == 15, 1.0, 0.0)
        mixture = jnp.zeros((width, tile), F32)
        for m in range(nspec):
            mixture = jnp.where(sub == m, weight_ref[m], mixture)

        def prepare(r, carry):
            u = state[r].astype(F32)
            inv = 1.0 / tau[pl.ds(r, 1), :]
            rho = jnp.sum(mixture * u, axis=0, keepdims=True) * inv
            gap = jnp.sum(relax * u, axis=0, keepdims=True) * inv
            coef[r] = gap * mixture + rho * relax
            return carry

        lax.fori_loop(0, rows, prepare, 0, unroll=4)

        def diagonal(vf):
            def one(r, carry):
                v = vf[r]
                change = jnp.sum(coef[r] * v, axis=0, keepdims=True)
                acc[r] = rate[pl.ds(r, 1), :] * v + relax * change
                return carry

            lax.fori_loop(0, rows, one, 0, unroll=4)

        diagonal(vf1)
        each(2, owners, send_higher)

        contract(0, rows, vf1)
        take_halo(0, vf1)
        contract(rows, rows + 2 * halo, vf1)
        link(0, w)
        first_block(0, w)

        def first_part(off, carry):
            q = source(off)
            pltpu.make_async_copy(got_meta.at[q], got_meta.at[q], meta_recv.at[order(q)]).wait()
            link(off, q)
            pltpu.make_async_copy(got.at[q], got.at[q], face_recv.at[order(q)]).wait()
            first_block(off, q)
            return carry

        lax.fori_loop(1, owners, first_part, 0)

        for h in range(halo):
            stage[1, 1, h] = acc[latest[halo_ref[0, 1, h]]].astype(BF16)
        for h in range(halo):
            stage[1, 0, h] = acc[latest[halo_ref[0, 0, h]]].astype(BF16)
        send_halo(1)
        for r in range(rows):
            value = acc[latest[r]]
            outv1[r] = value
            vf2[r] = value.astype(BF16).astype(F32)
        diagonal(vf2)
        contract(0, rows, vf2)

        def second_own(off, carry):
            for c in range(CAP):
                row = own_row[off * CAP + c]
                part[off * CAP + c] = applied(off, c, 0, row) + speed[off, pl.ds(c, 1), :] * vf2[row]
            assemble(off, source(off))
            return carry

        lax.fori_loop(0, owners, second_own, 0)
        pltpu.make_async_copy(faces.at[pl.ds(0, owners - 1)], faces.at[pl.ds(0, owners - 1)], face_send).wait()
        pltpu.make_async_copy(meta.at[pl.ds(0, owners - 1)], meta.at[pl.ds(0, owners - 1)], meta_send).wait()
        take_halo(1, vf2)

        def second_nbr(off, carry):
            for c in range(CAP):
                chain(off, c, part[off * CAP + c] + neighboured(off, c, vf2))
            return carry

        lax.fori_loop(0, owners, second_nbr, 0, unroll=4)
        for r in range(rows):
            outv2[r] = acc[latest[r]]
        settle(halo_send, stage, stage.at[0])

    dma = pltpu.SemaphoreType.DMA
    pl.run_scoped(scope, dma((13,)), dma(()), dma(()), dma(()))


def store(a, b, c, d):
    def run(sem):
        copies = [pltpu.make_async_copy(a, c, sem.at[0]), pltpu.make_async_copy(b, d, sem.at[1])]
        for copy in copies:
            copy.start()
        for copy in copies:
            copy.wait()

    pl.run_scoped(run, pltpu.SemaphoreType.DMA((2,)))


def solution(mesh):
    owners = mesh.shape["wide"]
    slabs = mesh.shape["slab"]

    def on_device(fo, fn, lin, quad, weight, state, tau, rate, res, dest, row, nbr, halo_list):
        count, width, tile = fo.shape
        rows = res.shape[0]
        halo = halo_list.shape[2]
        hbm = pl.BlockSpec(memory_space=pltpu.MemorySpace.HBM)
        vmem = pl.BlockSpec(memory_space=pltpu.MemorySpace.VMEM)
        dma = pltpu.SemaphoreType.DMA
        row_set = (rows, width, tile)
        products = pl.pallas_call(
            functools.partial(kernel, owners, slabs),
            out_shape=(pltpu.VMEM(row_set, F32), pltpu.VMEM(row_set, F32)),
            in_specs=[hbm] * 13,
            out_specs=(vmem, vmem),
            scratch_shapes=[
                pltpu.VMEM(fo.shape, BF16),
                pltpu.VMEM(fn.shape, BF16),
                pltpu.VMEM(lin.shape, F32),
                pltpu.VMEM(quad.shape, BF16),
                pltpu.VMEM(state.shape, BF16),
                pltpu.VMEM(tau.shape, F32),
                pltpu.VMEM(rate.shape, F32),
                pltpu.VMEM(row_set, F32),
                pltpu.VMEM((owners, CAP, 2, width, tile), BF16),
                pltpu.VMEM((owners, CAP, 2, width, tile), BF16),
                pltpu.VMEM((owners, 8, tile), F32),
                pltpu.SMEM((owners, 2 * CAP), jnp.int32),
                pltpu.SMEM((owners, 2 * CAP), jnp.int32),
                pltpu.VMEM((owners, CAP, 2, width, tile), F32),
                pltpu.VMEM((width * width, 3 * width), BF16),
                pltpu.VMEM((width * width, width), BF16),
                pltpu.VMEM((rows + 2 * halo, width * width, tile), F32),
                pltpu.VMEM((rows + 2 * halo, width, tile), F32),
                pltpu.VMEM((width, 2 * width), BF16),
                pltpu.VMEM((owners, CAP, width * width, tile), F32),
                pltpu.VMEM(row_set, F32),
                pltpu.VMEM((rows + 1 + owners * CAP, width, tile), F32),
                pltpu.VMEM((owners * CAP, width, tile), F32),
                pltpu.VMEM((rows + 2 * halo, width, tile), F32),
                pltpu.VMEM((rows + 2 * halo, width, tile), F32),
                pltpu.VMEM((2, 2, halo, width, tile), BF16),
                pltpu.VMEM((2, 2, halo, width, tile), BF16),
                dma((owners - 1,)),
                dma((owners - 1,)),
                dma((2,)),
                pltpu.SemaphoreType.REGULAR((owners - 1,)),
                pltpu.SemaphoreType.REGULAR,
                pltpu.SMEM(weight.shape, F32),
                pltpu.SMEM((count,), jnp.int32),
                pltpu.SMEM(row.shape, jnp.int32),
                pltpu.SMEM(nbr.shape, jnp.int32),
                pltpu.SMEM(halo_list.shape, jnp.int32),
                pltpu.SMEM((rows + 1,), jnp.int32),
                pltpu.SMEM((owners * CAP,), jnp.int32),
                pltpu.SMEM((owners * CAP,), jnp.int32),
                pltpu.SMEM((owners * CAP,), jnp.int32),
                pltpu.SMEM((owners, CAP), jnp.int32),
            ],
            compiler_params=pltpu.CompilerParams(collective_id=0, has_side_effects=True),
        )(fo, fn, lin, quad, weight, state, tau, rate, res, dest.reshape(count), row, nbr, halo_list)
        return pl.pallas_call(
            store,
            out_shape=(jax.ShapeDtypeStruct(row_set, F32), jax.ShapeDtypeStruct(row_set, F32)),
            in_specs=[vmem, vmem],
            out_specs=(hbm, hbm),
        )(*[pltpu.with_memory_space_constraint(x, pltpu.MemorySpace.VMEM) for x in products])

    every = ("slab", "wide")
    cube, flat = P(every, None, None), P(every, None)
    return jax.shard_map(
        on_device,
        mesh=mesh,
        in_specs=(cube, cube, P(), P(), P(), cube, flat, flat, cube, flat, P(every), P(every), cube),
        out_specs=(cube, cube),
        check_vma=False,
    )
```

```python
import functools

import jax
import jax.numpy as jnp
from jax import lax
from jax.experimental import pallas as pl
from jax.experimental.pallas import tpu as pltpu
from jax.sharding import PartitionSpec as P

CAP = 4
MESH = pl.DeviceIdType.MESH
F32 = jnp.float32
BF16 = jnp.bfloat16


def each(low, high, body):
    if high - low <= 8:
        for i in range(low, high):
            body(i)
    else:

        def step(i, carry):
            body(i)
            return carry

        lax.fori_loop(low, high, step, 0)


def kernel(
    owners,
    slabs,
    fo_hbm,
    fn_hbm,
    lin_hbm,
    quad_hbm,
    weight_hbm,
    state_hbm,
    tau_hbm,
    rate_hbm,
    res_hbm,
    dest_hbm,
    row_hbm,
    nbr_hbm,
    halo_hbm,
    outv1,
    outv2,
    fo,
    fn,
    lin,
    quad,
    state,
    tau,
    rate,
    res,
    faces,
    got,
    speed,
    meta,
    got_meta,
    uf,
    flux,
    form,
    bilinear,
    linear,
    flin,
    mats,
    coef,
    acc,
    part,
    vf1,
    vf2,
    stage,
    land,
    face_recv,
    meta_recv,
    halo_recv,
    ready,
    halo_ready,
    weight_ref,
    dest_ref,
    row_ref,
    nbr_ref,
    halo_ref,
    latest,
    before,
    own_row,
    nbr_row,
    picked,
):
    def scope(in_sem, face_send, meta_send, halo_send):
        s = lax.axis_index("slab")
        w = lax.axis_index("wide")
        count, width, tile = fo.shape
        rows = res.shape[0]
        nspec = weight_ref.shape[0]
        halo = halo_ref.shape[2]
        wide = width * width
        first_slot = rows + 1

        barrier = pltpu.get_barrier_semaphore()
        even = lax.rem(s, 2) == 0
        has_down = s > 0
        has_up = s < slabs - 1
        inner = has_down & has_up

        def signal(sem, slab, wide):
            pl.semaphore_signal(sem, inc=1, device_id=(slab, wide), device_id_type=MESH)

        def greet(off):
            @pl.when(w + off < owners)
            def _():
                signal(barrier, s, w + off)

        def answer(off):
            @pl.when(w - off >= 0)
            def _():
                signal(ready.at[w - 1], s, w - off)

        bits = count.bit_length()
        mask = (1 << bits) - 1

        def picks(peer):
            packed = jnp.int32(0)
            for t in range(count):
                packed = jnp.where(dest_ref[t] == peer, packed * (1 << bits) + (t + 1), packed)
            return [(packed >> (bits * c)) & mask for c in range(CAP)]

        def fill_meta(d, place):
            found = picks(d)
            for c in range(CAP):
                source = jnp.maximum(found[c] - 1, 0)
                picked[d, c] = source
                place[d, c] = jnp.where(found[c] > 0, row_ref[source], rows)
                place[d, CAP + c] = jnp.where(found[c] > 0, nbr_ref[source], 0)

        def fill_faces(d, place, low=0, some=CAP):
            for c in range(low, low + some):
                source = picked[d, c]
                place[d, c, 0] = fo[source]
                place[d, c, 1] = fn[source]

        def order(peer):
            return peer - jnp.where(peer > w, 1, 0)

        def face_copy(peer, c, some):
            return pltpu.make_async_remote_copy(
                src_ref=faces.at[peer, pl.ds(c, some)],
                dst_ref=got.at[w, pl.ds(c, some)],
                send_sem=face_send,
                recv_sem=face_recv.at[w - jnp.where(w > peer, 1, 0)],
                device_id=(s, peer),
                device_id_type=MESH,
            )

        def meta_copy(peer):
            return pltpu.make_async_remote_copy(
                src_ref=meta.at[peer],
                dst_ref=got_meta.at[w],
                send_sem=meta_send,
                recv_sem=meta_recv.at[w - jnp.where(w > peer, 1, 0)],
                device_id=(s, peer),
                device_id_type=MESH,
            )

        def name_lower(peer):
            @pl.when(peer < w)
            def _():
                fill_meta(peer, meta)
                meta_copy(peer).start()

        def send_lower(peer):
            @pl.when(peer < w)
            def _():
                for c in range(0, CAP, 2):
                    fill_faces(peer, faces, c, 2)
                    face_copy(peer, c, 2).start()

        def fill_higher(off):
            @pl.when(w + off < owners)
            def _():
                fill_meta(w + off, meta)
                fill_faces(w + off, faces)

        def send_higher(off):
            peer = w + off

            @pl.when(peer < owners)
            def _():
                pl.semaphore_wait(ready.at[peer - 1], 1)
                meta_copy(peer).start()
                for c in range(0, CAP, 2):
                    face_copy(peer, c, 2).start()

        def up_copy(phase, h, some):
            return pltpu.make_async_remote_copy(
                src_ref=stage.at[phase, 0, pl.ds(h, some)],
                dst_ref=land.at[phase, 0, pl.ds(h, some)],
                send_sem=halo_send,
                recv_sem=halo_recv.at[phase],
                device_id=(s + 1, w),
                device_id_type=MESH,
            )

        def down_copy(phase, h, some):
            return pltpu.make_async_remote_copy(
                src_ref=stage.at[phase, 1, pl.ds(h, some)],
                dst_ref=land.at[phase, 1, pl.ds(h, some)],
                send_sem=halo_send,
                recv_sem=halo_recv.at[phase],
                device_id=(s - 1, w),
                device_id_type=MESH,
            )

        def send_halo(phase):
            @pl.when(has_down)
            def _():
                for h in range(0, halo, 2):
                    down_copy(phase, h, min(2, halo - h)).start()

            @pl.when(has_up)
            def _():
                for h in range(0, halo, 2):
                    up_copy(phase, h, min(2, halo - h)).start()

        def settle(sem, many, few):
            @pl.when(inner)
            def _():
                pltpu.make_async_copy(many, many, sem).wait()

            @pl.when(jnp.logical_not(inner))
            def _():
                pltpu.make_async_copy(few, few, sem).wait()

        def take_halo(phase, vf):
            settle(halo_recv.at[phase], land.at[phase], land.at[phase, 0])

            @pl.when(has_down)
            def _():
                for h in range(halo):
                    vf[rows + h] = land[phase, 0, h].astype(F32)

            @pl.when(has_up)
            def _():
                for h in range(halo):
                    vf[rows + halo + h] = land[phase, 1, h].astype(F32)

        def link(off, q):
            named = [got_meta[q, c] for c in range(CAP)]
            at = first_slot + off * CAP
            for c in range(CAP):
                last = latest[named[c]]
                for e in range(c):
                    last = jnp.where(named[e] == named[c], at + e, last)
                before[off * CAP + c] = last
                own_row[off * CAP + c] = jnp.minimum(named[c], rows - 1)
                nbr_row[off * CAP + c] = got_meta[q, CAP + c]
            for r in range(rows):
                last = latest[r]
                for c in range(CAP):
                    last = jnp.where(named[c] == r, at + c, last)
                latest[r] = last

        def unpack(off, q):
            for c in range(CAP):
                own = got[q, c, 0].astype(F32)
                nbr = got[q, c, 1].astype(F32)
                uf[off, c, 0] = own
                uf[off, c, 1] = nbr
                square = jnp.sum(own * own + nbr * nbr, axis=0, keepdims=True)
                speed[off, pl.ds(c, 1), :] = 0.5 + 0.5 * jnp.sqrt(square * (0.5 / width))

        def contract(low, high, vf):
            def some(i, carry):
                at = low + 4 * i
                vectors = jnp.concatenate([vf[at + n].astype(BF16) for n in range(4)], axis=1)
                filled = jnp.dot(form[...], vectors, preferred_element_type=F32)
                flat = jnp.dot(flin[...], jnp.concatenate([vectors, vectors], axis=0), preferred_element_type=F32)
                for n in range(4):
                    bilinear[at + n] = filled[:, n * tile : (n + 1) * tile]
                    linear[at + n] = flat[:, n * tile : (n + 1) * tile]
                return carry

            lax.fori_loop(0, (high - low) // 4, some, 0)

        def folded(term, low, high):
            sums = [term(low + n) for n in range(4)]
            for n in range(low + 4, high):
                sums[n % 4] = sums[n % 4] + term(n)
            return (sums[0] + sums[1]) + (sums[2] + sums[3])

        def applied(off, c, side, row):
            def term(k):
                block = bilinear[row, k * width : (k + 1) * width, :]
                return block * jnp.broadcast_to(uf[off, c, side, pl.ds(k, 1), :], (width, tile))

            return linear[row] + folded(term, 0, width)

        def assemble(off, q):
            states = jnp.concatenate([got[q, c, 1] for c in range(CAP)], axis=1)
            ones = jnp.ones((2 * width, CAP * tile), BF16)
            grown = jnp.dot(flux[...], jnp.concatenate([states, ones], axis=0), preferred_element_type=F32)
            for c in range(CAP):
                mats[off, c] = grown[:, c * tile : (c + 1) * tile]

        def neighboured(off, c, vf):
            row = nbr_row[off * CAP + c]

            def term(j):
                block = mats[off, c, j * width : (j + 1) * width, :]
                return block * jnp.broadcast_to(vf[row, pl.ds(j, 1), :], (width, tile))

            return folded(term, 0, width) - speed[off, pl.ds(c, 1), :] * vf[row]

        def first_block(off, q):
            unpack(off, q)
            for c in range(CAP):
                row = jnp.minimum(got_meta[q, c], rows - 1)
                nbr = got_meta[q, CAP + c]
                jump = speed[off, pl.ds(c, 1), :] * (vf1[row] - vf1[nbr])
                chain(off, c, (applied(off, c, 0, row) + jump) + applied(off, c, 1, nbr))

        def source(off):
            near = jnp.minimum(w, owners - 1 - w)
            apart = jnp.where(off <= 2 * near, (off + 1) // 2, off - near)
            below = jnp.where(off <= 2 * near, lax.rem(off, 2) == 1, 2 * w >= owners)
            return jnp.where(below, w - apart, w + apart)

        def chain(off, c, term):
            acc[first_slot + off * CAP + c] = term + acc[before[off * CAP + c]]

        def run():
            loads = [
                pltpu.make_async_copy(a, b, in_sem.at[i])
                for i, (a, b) in enumerate(
                    (
                        (dest_hbm, dest_ref),
                        (row_hbm, row_ref),
                        (nbr_hbm, nbr_ref),
                        (fo_hbm, fo),
                        (fn_hbm, fn),
                        (halo_hbm, halo_ref),
                        (res_hbm, res),
                        (quad_hbm, quad),
                        (lin_hbm, lin),
                        (state_hbm, state),
                        (tau_hbm, tau),
                        (rate_hbm, rate),
                        (weight_hbm, weight_ref),
                    )
                )
            ]
            for load in loads[:5]:
                load.start()
            each(1, owners, greet)

            @pl.when(jnp.logical_not(even))
            def _():
                signal(barrier, s - 1, w)

                @pl.when(has_up)
                def _():
                    signal(barrier, s + 1, w)

            for load in loads[5:]:
                load.start()
            around = jnp.where(has_down, 1, 0) + jnp.where(has_up, 1, 0)
            greeted = w + jnp.where(even, around, 0)

            @pl.when(greeted > 0)
            def _():
                pl.semaphore_wait(barrier, greeted)

            each(1, owners, answer)

            @pl.when(even)
            def _():
                @pl.when(has_down)
                def _():
                    signal(halo_ready, s - 1, w)

                @pl.when(has_up)
                def _():
                    signal(halo_ready, s + 1, w)

            for load in loads[:3]:
                load.wait()
            name_lower(0)
            for load in loads[3:5]:
                load.wait()
            send_lower(0)

            def next_lower(peer):
                name_lower(peer)
                send_lower(peer)

            each(1, owners - 1, next_lower)

            loads[5].wait()
            loads[6].wait()

            def round_rows(r, carry):
                vf1[r] = res[r].astype(BF16).astype(F32)
                return carry

            lax.fori_loop(0, rows, round_rows, 0, unroll=4)
            for h in range(halo):
                stage[0, 0, h] = vf1[halo_ref[0, 0, h]].astype(BF16)
                stage[0, 1, h] = vf1[halo_ref[0, 1, h]].astype(BF16)

            @pl.when(even)
            def _():
                send_halo(0)

            each(1, owners, fill_higher)
            fill_meta(w, got_meta)
            fill_faces(w, got)
            send_higher(1)

            for r in range(rows + 1):
                latest[r] = r
            acc[rows] = jnp.zeros((width, tile), F32)
            for vf in (vf1, vf2):

                @pl.when(s == 0)
                def _():
                    vf[pl.ds(rows, halo)] = jnp.zeros((halo, width, tile), F32)

                @pl.when(s == slabs - 1)
                def _():
                    vf[pl.ds(rows + halo, halo)] = jnp.zeros((halo, width, tile), F32)

            loads[7].wait()
            loads[8].wait()
            at = lax.broadcasted_iota(jnp.int32, (wide, wide), 0)
            column = lax.broadcasted_iota(jnp.int32, (wide, wide), 1)
            swap = jnp.where(column == lax.rem(at, width) * width + at // width, 1.0, 0.0).astype(BF16)
            flux[:, :width] = (
                lax.dot_general(swap, quad[...], (((1,), (1,)), ((), ())), preferred_element_type=F32) * 0.5
            ).astype(BF16)
            half_lin = lin[...] * 0.5
            high = half_lin.astype(BF16)
            low = (half_lin - high.astype(F32)).astype(BF16)
            at = lax.broadcasted_iota(jnp.int32, (wide, width), 0)
            column = lax.broadcasted_iota(jnp.int32, (wide, width), 1)
            pick = jnp.where(column == lax.rem(at, width), 1.0, 0.0).astype(BF16)
            keep = column == at // width
            flin[:, :width] = high
            flin[:, width:] = low
            for i, term in enumerate((high, low)):
                flux[:, (1 + i) * width : (2 + i) * width] = jnp.where(
                    keep, jnp.dot(pick, term, preferred_element_type=F32), 0.0
                ).astype(BF16)
            repeat = jnp.where(column == at // width, 1.0, 0.0).astype(BF16)
            each_state = jnp.dot(repeat, quad[...], preferred_element_type=F32) * 0.5
            at = lax.broadcasted_iota(jnp.int32, (wide, wide), 0)
            column = lax.broadcasted_iota(jnp.int32, (wide, wide), 1)
            each_state = jnp.where(column // width == lax.rem(at, width), each_state, 0.0).astype(BF16)
            at = lax.broadcasted_iota(jnp.int32, (wide, width), 0)
            column = lax.broadcasted_iota(jnp.int32, (wide, width), 1)
            gather = jnp.where(column == lax.rem(at, width), 1.0, 0.0).astype(BF16)
            form[...] = jnp.dot(each_state, gather, preferred_element_type=F32).astype(BF16)

            @pl.when(jnp.logical_not(even))
            def _():
                pl.semaphore_wait(halo_ready, around)
                send_halo(0)

            for load in loads[9:]:
                load.wait()

        run()

        sub = lax.broadcasted_iota(jnp.int32, (width, tile), 0)
        relax = jnp.where(sub == 14, 1.0, 0.0) - jnp.where(sub == 15, 1.0, 0.0)
        mixture = jnp.zeros((width, tile), F32)
        for m in range(nspec):
            mixture = jnp.where(sub == m, weight_ref[m], mixture)

        def prepare(r, carry):
            u = state[r].astype(F32)
            inv = 1.0 / tau[pl.ds(r, 1), :]
            rho = jnp.sum(mixture * u, axis=0, keepdims=True) * inv
            gap = jnp.sum(relax * u, axis=0, keepdims=True) * inv
            coef[r] = gap * mixture + rho * relax
            return carry

        lax.fori_loop(0, rows, prepare, 0, unroll=4)

        def diagonal(vf):
            def one(r, carry):
                v = vf[r]
                change = jnp.sum(coef[r] * v, axis=0, keepdims=True)
                acc[r] = rate[pl.ds(r, 1), :] * v + relax * change
                return carry

            lax.fori_loop(0, rows, one, 0, unroll=4)

        diagonal(vf1)
        each(2, owners, send_higher)

        contract(0, rows, vf1)
        take_halo(0, vf1)
        contract(rows, rows + 2 * halo, vf1)
        link(0, w)
        first_block(0, w)

        def first_part(off, carry):
            q = source(off)
            pltpu.make_async_copy(got_meta.at[q], got_meta.at[q], meta_recv.at[order(q)]).wait()
            link(off, q)
            pltpu.make_async_copy(got.at[q], got.at[q], face_recv.at[order(q)]).wait()
            first_block(off, q)
            return carry

        lax.fori_loop(1, owners, first_part, 0)

        for h in range(halo):
            stage[1, 1, h] = acc[latest[halo_ref[0, 1, h]]].astype(BF16)
        for h in range(halo):
            stage[1, 0, h] = acc[latest[halo_ref[0, 0, h]]].astype(BF16)
        send_halo(1)
        for r in range(rows):
            value = acc[latest[r]]
            outv1[r] = value
            vf2[r] = value.astype(BF16).astype(F32)
        diagonal(vf2)
        contract(0, rows, vf2)

        def second_own(off, carry):
            for c in range(CAP):
                row = own_row[off * CAP + c]
                part[off * CAP + c] = applied(off, c, 0, row) + speed[off, pl.ds(c, 1), :] * vf2[row]
            assemble(off, source(off))
            return carry

        lax.fori_loop(0, owners, second_own, 0)
        pltpu.make_async_copy(faces.at[pl.ds(0, owners - 1)], faces.at[pl.ds(0, owners - 1)], face_send).wait()
        pltpu.make_async_copy(meta.at[pl.ds(0, owners - 1)], meta.at[pl.ds(0, owners - 1)], meta_send).wait()
        take_halo(1, vf2)

        def second_nbr(off, carry):
            for c in range(CAP):
                chain(off, c, part[off * CAP + c] + neighboured(off, c, vf2))
            return carry

        lax.fori_loop(0, owners, second_nbr, 0, unroll=4)
        for r in range(rows):
            outv2[r] = acc[latest[r]]
        settle(halo_send, stage, stage.at[0])

    dma = pltpu.SemaphoreType.DMA
    pl.run_scoped(scope, dma((13,)), dma(()), dma(()), dma(()))


def store(a, b, c, d):
    def run(sem):
        copies = [pltpu.make_async_copy(a, c, sem.at[0]), pltpu.make_async_copy(b, d, sem.at[1])]
        for copy in copies:
            copy.start()
        for copy in copies:
            copy.wait()

    pl.run_scoped(run, pltpu.SemaphoreType.DMA((2,)))


def solution(mesh):
    owners = mesh.shape["wide"]
    slabs = mesh.shape["slab"]

    def on_device(fo, fn, lin, quad, weight, state, tau, rate, res, dest, row, nbr, halo_list):
        count, width, tile = fo.shape
        rows = res.shape[0]
        halo = halo_list.shape[2]
        hbm = pl.BlockSpec(memory_space=pltpu.MemorySpace.HBM)
        vmem = pl.BlockSpec(memory_space=pltpu.MemorySpace.VMEM)
        dma = pltpu.SemaphoreType.DMA
        row_set = (rows, width, tile)
        products = pl.pallas_call(
            functools.partial(kernel, owners, slabs),
            out_shape=(pltpu.VMEM(row_set, F32), pltpu.VMEM(row_set, F32)),
            in_specs=[hbm] * 13,
            out_specs=(vmem, vmem),
            scratch_shapes=[
                pltpu.VMEM(fo.shape, BF16),
                pltpu.VMEM(fn.shape, BF16),
                pltpu.VMEM(lin.shape, F32),
                pltpu.VMEM(quad.shape, BF16),
                pltpu.VMEM(state.shape, BF16),
                pltpu.VMEM(tau.shape, F32),
                pltpu.VMEM(rate.shape, F32),
                pltpu.VMEM(row_set, F32),
                pltpu.VMEM((owners, CAP, 2, width, tile), BF16),
                pltpu.VMEM((owners, CAP, 2, width, tile), BF16),
                pltpu.VMEM((owners, 8, tile), F32),
                pltpu.SMEM((owners, 2 * CAP), jnp.int32),
                pltpu.SMEM((owners, 2 * CAP), jnp.int32),
                pltpu.VMEM((owners, CAP, 2, width, tile), F32),
                pltpu.VMEM((width * width, 3 * width), BF16),
                pltpu.VMEM((width * width, width), BF16),
                pltpu.VMEM((rows + 2 * halo, width * width, tile), F32),
                pltpu.VMEM((rows + 2 * halo, width, tile), F32),
                pltpu.VMEM((width, 2 * width), BF16),
                pltpu.VMEM((owners, CAP, width * width, tile), F32),
                pltpu.VMEM(row_set, F32),
                pltpu.VMEM((rows + 1 + owners * CAP, width, tile), F32),
                pltpu.VMEM((owners * CAP, width, tile), F32),
                pltpu.VMEM((rows + 2 * halo, width, tile), F32),
                pltpu.VMEM((rows + 2 * halo, width, tile), F32),
                pltpu.VMEM((2, 2, halo, width, tile), BF16),
                pltpu.VMEM((2, 2, halo, width, tile), BF16),
                dma((owners - 1,)),
                dma((owners - 1,)),
                dma((2,)),
                pltpu.SemaphoreType.REGULAR((owners - 1,)),
                pltpu.SemaphoreType.REGULAR,
                pltpu.SMEM(weight.shape, F32),
                pltpu.SMEM((count,), jnp.int32),
                pltpu.SMEM(row.shape, jnp.int32),
                pltpu.SMEM(nbr.shape, jnp.int32),
                pltpu.SMEM(halo_list.shape, jnp.int32),
                pltpu.SMEM((rows + 1,), jnp.int32),
                pltpu.SMEM((owners * CAP,), jnp.int32),
                pltpu.SMEM((owners * CAP,), jnp.int32),
                pltpu.SMEM((owners * CAP,), jnp.int32),
                pltpu.SMEM((owners, CAP), jnp.int32),
            ],
            compiler_params=pltpu.CompilerParams(collective_id=0, has_side_effects=True),
        )(fo, fn, lin, quad, weight, state, tau, rate, res, dest.reshape(count), row, nbr, halo_list)
        return pl.pallas_call(
            store,
            out_shape=(jax.ShapeDtypeStruct(row_set, F32), jax.ShapeDtypeStruct(row_set, F32)),
            in_specs=[vmem, vmem],
            out_specs=(hbm, hbm),
        )(*[pltpu.with_memory_space_constraint(x, pltpu.MemorySpace.VMEM) for x in products])

    every = ("slab", "wide")
    cube, flat = P(every, None, None), P(every, None)
    return jax.shard_map(
        on_device,
        mesh=mesh,
        in_specs=(cube, cube, P(), P(), P(), cube, flat, flat, cube, flat, P(every), P(every), cube),
        out_specs=(cube, cube),
        check_vma=False,
    )
```
